256 devices in a mesh: tmpl: 32 (over z_lo, y, x), sta: 8 (over z_hi, core).
Axes of the slice: x: 4, y: 4, z: 8 (z_hi: 4, z_lo: 2; z = z_hi * 2 + z_lo), core: 2. Of those that a mesh axis runs over, the one named last changes fastest.
Arguments:
- records: float32 [152, 4096], P('sta', 'tmpl'), may hold values from -6 to 6
- templates: float32 [128, 152, 600], P('tmpl', 'sta'), may hold values from -6 to 6
- offsets: int32 [128, 152], P('tmpl', 'sta'), may hold values from 0 to 425
- available: int32 [128, 152], P('tmpl', 'sta'), may hold values 0 or 1
Outputs:
- detection: float32 [128, 3072], P('tmpl', 'sta')
The draws below stay inside these ranges and needn't reach their ends.
All inputs are finite; a program needn't handle non-finite values. No bound on the sum of `available` on one device may be relied on, other than what follows from the above.
Results may differ from the reference program's by a relative error of at most 0.0066.
Values may be sent and summed in bfloat16 or wider, within the bound.
No kernel may reach another device: no remote copies, remote signals or barrier semaphores. Data moves between devices by JAX's collectives and lax.ppermute only.
A program may use at most 64 MiB of HBM per device.

```python
import math
import jax
import jax.numpy as jnp
from jax import lax

CHANNELS = 152
TSAMP = 600
OFFMAX = 425
TEMPLATES = 128
NT = 4096
NLAG = 3072


def draw_records(key, part):
    base_key = jax.random.fold_in(key, 101)
    noise_key, level_key = jax.random.split(base_key, 2)
    offset_level = jax.random.uniform(level_key, (CHANNELS, 1), jnp.float32, -2.0, 2.0)
    drawn_values = offset_level + jax.random.normal(noise_key, (CHANNELS, NT), jnp.float32)
    return jnp.clip(drawn_values, -6.0, 6.0)


def draw_templates(key, part):
    base_key = jax.random.fold_in(key, 202)
    noise_key, level_key = jax.random.split(base_key, 2)
    offset_level = jax.random.uniform(level_key, (TEMPLATES, CHANNELS, 1), jnp.float32, -2.0, 2.0)
    drawn_values = offset_level + jax.random.normal(noise_key, (TEMPLATES, CHANNELS, TSAMP), jnp.float32)
    return jnp.clip(drawn_values, -6.0, 6.0)


def place_ends(array, rng, least, high):
    index_at = [jax.random.randint(jax.random.fold_in(rng, axis), (), 0, length) for axis, length in enumerate(array.shape)]
    widest = array.shape.index(max(array.shape))
    beside = index_at[:widest] + [(index_at[widest] + 1) % array.shape[widest]] + index_at[widest + 1:]
    return array.at[tuple(index_at)].set(least).at[tuple(beside)].set(high)


def setup_inputs(seed: int = 0) -> dict:
    seeds = jax.random.split(jax.random.key(seed), 5)
    records = draw_records(jax.random.fold_in(seeds[4], 71), 0)
    templates = draw_templates(jax.random.fold_in(seeds[4], 71), 0)
    offsets = place_ends(jax.random.randint(seeds[2], (TEMPLATES, CHANNELS), 0, OFFMAX + 1), jax.random.fold_in(seeds[2], 1), 0, OFFMAX).astype(jnp.int32)
    available = place_ends((jax.random.randint(seeds[3], (TEMPLATES, CHANNELS), 0, 4) < 3).astype(jnp.int32), jax.random.fold_in(seeds[3], 1), 0, 1)
    return {"records": records, "templates": templates, "offsets": offsets, "available": available}


def scale_from(running, squared, length, positions):
    first = running[:, length:length + positions] - running[:, :positions]
    second = squared[:, length:length + positions] - squared[:, :positions]
    energy = second - first * first / length
    return 1.0 / jnp.sqrt(energy + 1e-05)

def framed(records_low, count, width, step):
    pieces = width // step
    total = (count + pieces - 1) * step
    padded = jnp.pad(records_low, ((0, 0), (0, total - records_low.shape[1])))
    rows_cut = padded.reshape(records_low.shape[0], count + pieces - 1, step)
    frames = jnp.stack([rows_cut[:, piece:piece + count] for piece in range(pieces)], axis=2)
    return frames.reshape(records_low.shape[0], count, width)

def shifted_copies(centred_low, width, step):
    length = centred_low.shape[2]
    padded = jnp.pad(centred_low, ((0, 0), (0, 0), (0, width + 1 - length)))
    tiled = jnp.tile(padded, (1, 1, step))[:, :, :step * width]
    return tiled.reshape(centred_low.shape[0], centred_low.shape[1], step, width)

def pick_lags(values, starts, count):
    return jax.vmap(jax.vmap(lambda series, start: lax.dynamic_slice_in_dim(series, start, count)))(values, starts)

def reference(records, templates, offsets, available):
    positions = NLAG + OFFMAX
    step = 32
    width = step * ((TSAMP + 2 * step - 2) // step)
    count = (positions + step - 1) // step
    anchor = jnp.zeros((records.shape[0], 1), records.dtype)
    running = jnp.concatenate([anchor, jnp.cumsum(records, axis=1)], axis=1)
    squared = jnp.concatenate([anchor, jnp.cumsum(records * records, axis=1)], axis=1)
    scale = scale_from(running, squared, TSAMP, positions)
    frames = framed(records.astype(jnp.bfloat16), count, width, step).astype(jnp.float32)
    group_size = math.gcd(TEMPLATES, 4)
    groups = TEMPLATES // group_size

    def stack_group(inputs):
        shapes, starts, present = inputs
        centred = shapes - lax.optimization_barrier(jnp.mean(shapes, axis=2, keepdims=True))
        norms = jnp.sqrt(lax.optimization_barrier(jnp.sum(centred * centred, axis=2)) + 1e-05)
        copies = shifted_copies(centred.astype(jnp.bfloat16), width, step).astype(jnp.float32)
        correlated = jnp.einsum('tcsw,cbw->tcbs', copies, frames, precision=lax.Precision.HIGHEST)
        correlated = correlated.reshape(group_size, CHANNELS, count * step)[:, :, :positions]
        picked = pick_lags(correlated * scale[None], starts, NLAG)
        return lax.optimization_barrier(jnp.sum(picked * (present.astype(jnp.float32) / norms)[:, :, None], axis=1))
    stack = lax.map(stack_group, (templates.reshape(groups, group_size, CHANNELS, TSAMP), offsets.reshape(groups, group_size, CHANNELS).astype(jnp.int32), available.reshape(groups, group_size, CHANNELS)))
    stack = stack.reshape(TEMPLATES, NLAG)
    power = lax.optimization_barrier(jnp.mean(stack * stack, axis=1, keepdims=True))
    return stack / jnp.sqrt(power + 1e-05)
```

```python
import jax
import jax.numpy as jnp
from jax import lax
from jax.experimental import pallas as pl
from jax.experimental.pallas import tpu as pltpu
from jax.sharding import PartitionSpec as P

LANES = 128


def stack_kernel(off_ref, avail_ref, records_ref, templates_ref, out_ref, pad_ref, rev_ref, inv_ref, pieces_ref, sums_ref, moved_ref, acc_ref):
    templ_here, channels_here, length = templates_ref.shape
    blocks = records_ref.shape[0]
    taps = rev_ref.shape[2] // LANES
    lag_blocks = acc_ref.shape[1]
    bf16, f32 = jnp.bfloat16, jnp.float32

    row = lax.broadcasted_iota(jnp.int32, (LANES, LANES), 0)
    col = lax.broadcasted_iota(jnp.int32, (LANES, LANES), 1)
    flip = (row + col == LANES - 1).astype(f32).astype(bf16)
    pad_ref[...] = jnp.zeros_like(pad_ref)
    for t in range(templ_here):
        shapes = templates_ref[t]
        centred = shapes - jnp.sum(shapes, axis=1, keepdims=True) / length
        energy = jnp.sum(centred * centred, axis=1, keepdims=True)
        inv_ref[t] = jnp.broadcast_to(lax.rsqrt(energy + 1e-05), (channels_here, LANES))
        pad_ref[:, :length] = centred
        for q in range(taps):
            block = pad_ref[:, q * LANES : (q + 1) * LANES].astype(bf16)
            rev_ref[t, :, (taps - 1 - q) * LANES : (taps - q) * LANES] = jnp.dot(
                block, flip, preferred_element_type=f32
            )

    for c in range(channels_here):
        x = records_ref[:, c * LANES : (c + 1) * LANES]
        for k, v in enumerate((x, x * x)):
            rows = pl.ds((2 * c + k) * blocks, blocks)
            high = v.astype(bf16)
            rest = v - high.astype(f32)
            mid = rest.astype(bf16)
            low = (rest - mid.astype(f32)).astype(bf16)
            pieces_ref[rows, 0:LANES] = high
            pieces_ref[rows, LANES : 2 * LANES] = mid
            pieces_ref[rows, 2 * LANES : 3 * LANES] = low
    tail = (row >= col).astype(f32)
    adder = jnp.concatenate([tail, jnp.ones_like(tail)], axis=1).astype(bf16)
    adder = jnp.concatenate([adder, adder, adder], axis=0)
    sums = jnp.dot(pieces_ref[...], adder, preferred_element_type=f32)
    sums_ref[:, :blocks, :] = sums.reshape(2 * channels_here, blocks, 2 * LANES)
    sums_ref[:, blocks:, :] = jnp.zeros((2 * channels_here, sums_ref.shape[1] - blocks, 2 * LANES), f32)
    acc_ref[...] = jnp.zeros_like(acc_ref)

    whole = length // LANES
    left = length % LANES
    turn = LANES - left
    lane = lax.broadcasted_iota(jnp.int32, (blocks, LANES), 1)
    lag_lane = lax.broadcasted_iota(jnp.int32, (lag_blocks, LANES), 1)

    def window_sum(index):
        def at(i, k):
            return sums_ref[index, i : i + blocks, k * LANES : (k + 1) * LANES]

        total = at(0, 0)
        for i in range(1, whole + 1):
            total = total + at(i, 1)
        ends = jnp.where(lane < turn, 0.0, at(whole + 1, 1))
        near = pltpu.roll(at(whole, 0), turn, 1)
        far = pltpu.roll(at(whole + 1, 0), turn, 1)
        return total + (ends - jnp.where(lane < turn, near, far))

    def channel(c, carry):
        first = window_sum(2 * c)
        second = window_sum(2 * c + 1)
        scale = lax.rsqrt(second - first * first / length + 1e-05)

        x = records_ref[:, pl.ds(pl.multiple_of(c * LANES, LANES), LANES)]
        moved_ref[0, :blocks, :] = x
        moved_ref[0, blocks:, :] = jnp.zeros((moved_ref.shape[1] - blocks, LANES), f32)
        frames = jnp.concatenate(
            [moved_ref[0, q : q + blocks, :].astype(bf16) for q in range(taps)], axis=1
        )
        weights = []
        for t in range(templ_here):
            line = jnp.broadcast_to(rev_ref[t, pl.ds(c, 1), :], (LANES, taps * LANES))
            turned = pltpu.roll(line, (taps - 1) * LANES + 1, 1, stride=1, stride_axis=0).astype(bf16)
            weights.append(
                jnp.concatenate(
                    [turned[:, (taps - 1 - q) * LANES : (taps - q) * LANES] for q in range(taps)], axis=0
                )
            )
        correlated = jnp.dot(frames, jnp.concatenate(weights, axis=1), preferred_element_type=f32)
        for t in range(templ_here):
            start = off_ref[t, c]
            down = start // LANES
            over = start % LANES
            scaled = correlated[:, t * LANES : (t + 1) * LANES] * scale
            moved_ref[1 + t, :blocks, :] = pltpu.roll(scaled, (LANES - over) % LANES, 1)
            here = moved_ref[1 + t, pl.ds(down, lag_blocks), :]
            after = moved_ref[1 + t, pl.ds(down + 1, lag_blocks), :]
            picked = jnp.where(lag_lane < LANES - over, here, after)
            weight = inv_ref[t, pl.ds(c, 1), :] * avail_ref[t, c].astype(f32)
            acc_ref[t] += picked * weight
        return carry

    lax.fori_loop(0, channels_here, channel, 0)
    share = out_ref.shape[1] // templ_here
    for g in range(out_ref.shape[0]):
        for t in range(templ_here):
            out_ref[g, t * share : (t + 1) * share, :] = acc_ref[t, g * share : (g + 1) * share, :]


def partial_stacks(blocks, templates, offsets, available, lag_count, shares):
    count = blocks.shape[0]
    templ_here, channels_here, length = templates.shape
    taps = (length + 2 * LANES - 2) // LANES
    lag_blocks = lag_count // LANES
    f32 = jnp.float32
    smem = pl.BlockSpec(memory_space=pltpu.SMEM)
    vmem = pl.BlockSpec(memory_space=pltpu.VMEM)
    total_rows = 2 * channels_here * count
    return pl.pallas_call(
        stack_kernel,
        out_shape=jax.ShapeDtypeStruct((shares, templ_here * lag_blocks // shares, LANES), f32),
        in_specs=[smem, smem, vmem, vmem],
        out_specs=vmem,
        scratch_shapes=[
            pltpu.VMEM((channels_here, taps * LANES), f32),
            pltpu.VMEM((templ_here, channels_here, taps * LANES), f32),
            pltpu.VMEM((templ_here, channels_here, LANES), f32),
            pltpu.VMEM((total_rows, 3 * LANES), jnp.bfloat16),
            pltpu.VMEM((2 * channels_here, count + 8, 2 * LANES), f32),
            pltpu.VMEM((1 + templ_here, count + 8, LANES), f32),
            pltpu.VMEM((templ_here, lag_blocks, LANES), f32),
        ],
        compiler_params=pltpu.CompilerParams(vmem_limit_bytes=32 << 20),
        name="stack_channels",
    )(offsets, available, blocks, templates)


OFFMAX = 425


def shards(records, templates, offsets, available):
    channels_here, block_len = records.shape
    templ_here, _, length = templates.shape
    count = lax.axis_size("tmpl")
    shares = lax.axis_size("sta")
    lag_count = block_len * count - OFFMAX - length + 1
    mine = jnp.broadcast_to(records.reshape(1, channels_here * block_len), (count, channels_here * block_len))
    blocks = lax.all_to_all(mine, "tmpl", 0, 0, tiled=True)
    parts = partial_stacks(blocks, templates, offsets, available, lag_count, shares)
    parts = lax.all_to_all(parts, "sta", 0, 0, tiled=True)
    stack = jnp.sum(parts, axis=0).reshape(templ_here, lag_count // shares)
    power = lax.psum(jnp.sum(stack * stack, axis=1, keepdims=True), "sta") / lag_count
    return stack / jnp.sqrt(power + 1e-05)


def solution(mesh):
    in_specs = (P("sta", "tmpl"), P("tmpl", "sta", None), P("tmpl", "sta"), P("tmpl", "sta"))
    out_specs = P("tmpl", "sta")
    return jax.shard_map(shards, mesh=mesh, in_specs=in_specs, out_specs=out_specs, check_vma=False)
```

```python
import jax
import jax.numpy as jnp
from jax import lax
from jax.experimental import pallas as pl
from jax.experimental.pallas import tpu as pltpu
from jax.sharding import PartitionSpec as P

OFFMAX = 425
LANES = 128
SUBLANES = 8
SLOTS = 4
SMEM = pl.BlockSpec(memory_space=pltpu.SMEM)
VMEM = pl.BlockSpec(memory_space=pltpu.VMEM)
HBM = pl.BlockSpec(memory_space=pltpu.HBM)


def padded_rows(rows):
    return -(-rows // SUBLANES) * SUBLANES


def chunks_of(length, step):
    return (length + 2 * step - 2) // step


def limit(mib):
    return pltpu.CompilerParams(vmem_limit_bytes=mib << 20)


def spread_kernel(records_ref, out_ref, sem):
    channels = pl.ds(0, records_ref.shape[0])
    copies = [pltpu.make_async_copy(records_ref, out_ref.at[i, channels], sem.at[i]) for i in range(out_ref.shape[0])]
    for copy in copies:
        copy.start()
    for copy in copies:
        copy.wait()


def weights_kernel(templates_ref, weights_ref, inv_ref, lines_ref, chunks_ref):
    templ_here, channels_here, length = templates_ref.shape
    step = LANES // templ_here
    chunks = weights_ref.shape[1] // step
    groups = lines_ref.shape[0]
    width = templ_here * LANES
    bf16, f32 = jnp.bfloat16, jnp.float32
    lines_ref[...] = jnp.zeros_like(lines_ref)
    for t in range(templ_here):
        shapes = templates_ref[t]
        centred = shapes - jnp.sum(shapes, axis=1, keepdims=True) / length
        energy = jnp.sum(centred * centred, axis=1, keepdims=True)
        inv_ref[t] = jnp.broadcast_to(lax.rsqrt(energy + 1e-05), (channels_here, LANES))
        for q in range(groups):
            here = min(LANES, length - q * LANES)
            lines_ref[q, :channels_here, t * LANES : t * LANES + here] = centred[:, q * LANES : q * LANES + here]
    col = lax.broadcasted_iota(jnp.int32, (1, width), 1)
    source = LANES * ((col % LANES) // step) + step * (col // LANES) + step - 1 - col % step
    pick = (lax.broadcasted_iota(jnp.int32, (width, width), 0) == source).astype(f32).astype(bf16)
    lines = lines_ref[...].reshape(groups * lines_ref.shape[1], width).astype(bf16)
    picked = jnp.dot(lines, pick, preferred_element_type=f32)
    rows = lines_ref.shape[1]
    for m in range(chunks_ref.shape[0]):
        q, i = divmod(m, templ_here)
        chunks_ref[m] = picked[q * rows : (q + 1) * rows, i * LANES : (i + 1) * LANES]

    row = lax.broadcasted_iota(jnp.int32, (step, LANES), 0)
    inside = lax.broadcasted_iota(jnp.int32, (step, LANES), 1) % step <= row

    def channel(c, carry):
        before = jnp.zeros((step, LANES), f32)
        for m in range(chunks):
            if m * step < length:
                line = jnp.broadcast_to(chunks_ref[m, pl.ds(c, 1), :], (step, LANES))
                here = pltpu.roll(line, LANES - step + 1, 1, stride=1, stride_axis=0)
                following = pltpu.roll(line, 1, 1, stride=1, stride_axis=0)
            else:
                here = following = jnp.zeros((step, LANES), f32)
            weights_ref[c, m * step : (m + 1) * step, :] = jnp.where(inside, here, before).astype(bf16)
            before = following
        return carry

    lax.fori_loop(0, channels_here, channel, 0)


def stack_kernel(
    off_hbm, avail_hbm, records_ref, weights_ref, inv_ref, out_ref,
    off_ref, avail_ref, pieces_ref, sums_ref, framed_ref, moved_ref, acc_ref, sem,
    *, length,
):
    templ_here, channels_here, _ = inv_ref.shape
    step = LANES // templ_here
    blocks = framed_ref.shape[2] - SUBLANES
    pitch = records_ref.shape[0] // blocks
    lag_blocks = acc_ref.shape[1] // 2
    taps = weights_ref.shape[1] // LANES
    bf16, f32 = jnp.bfloat16, jnp.float32
    small = [pltpu.make_async_copy(off_hbm, off_ref, sem.at[0]), pltpu.make_async_copy(avail_hbm, avail_ref, sem.at[1])]
    for copy in small:
        copy.start()

    for c in range(channels_here):
        x = records_ref[pl.ds(c, blocks, stride=pitch), :]
        for k, v in enumerate((x, x * x)):
            rows = pl.ds((2 * c + k) * blocks, blocks)
            high = v.astype(bf16)
            rest = v - high.astype(f32)
            mid = rest.astype(bf16)
            low = (rest - mid.astype(f32)).astype(bf16)
            pieces_ref[rows, 0:LANES] = high
            pieces_ref[rows, LANES : 2 * LANES] = mid
            pieces_ref[rows, 2 * LANES : 3 * LANES] = low
    row = lax.broadcasted_iota(jnp.int32, (LANES, LANES), 0)
    col = lax.broadcasted_iota(jnp.int32, (LANES, LANES), 1)
    tail = (row >= col).astype(f32)
    adder = jnp.concatenate([tail, jnp.ones_like(tail)], axis=1).astype(bf16)
    adder = jnp.concatenate([adder, adder, adder], axis=0)
    sums = jnp.dot(pieces_ref[...], adder, preferred_element_type=f32)
    sums_ref[:, :blocks, :] = sums.reshape(2 * channels_here, blocks, 2 * LANES)
    sums_ref[:, blocks:, :] = jnp.zeros((2 * channels_here, SUBLANES, 2 * LANES), f32)
    acc_ref[...] = jnp.zeros_like(acc_ref)
    framed_ref[:, :, blocks:, :] = jnp.zeros((*framed_ref.shape[:2], SUBLANES, LANES), f32)
    for copy in small:
        copy.wait()

    whole = length // LANES
    turn = LANES - length % LANES
    lane = lax.broadcasted_iota(jnp.int32, (blocks, LANES), 1)
    lag_lane = lax.broadcasted_iota(jnp.int32, (lag_blocks, LANES), 1)

    def window_sum(index):
        def at(i, k):
            return sums_ref[index, i : i + blocks, k * LANES : (k + 1) * LANES]

        total = at(0, 0)
        for i in range(1, whole + 1):
            total = total + at(i, 1)
        ends = jnp.where(lane < turn, 0.0, at(whole + 1, 1))
        near = pltpu.roll(at(whole, 0), turn, 1)
        far = pltpu.roll(at(whole + 1, 0), turn, 1)
        return total + (ends - jnp.where(lane < turn, near, far))

    def regroup(arrays, group):
        count = len(arrays)
        distance = 1
        while distance < count:
            kept = (lane // group) // distance % 2 == 0
            swapped = list(arrays)
            for r in range(count):
                if r // distance % 2 == 0:
                    a, b = arrays[r], arrays[r + distance]
                    shift = group * distance
                    swapped[r] = jnp.where(kept, a, pltpu.roll(b, shift, 1))
                    swapped[r + distance] = jnp.where(kept, pltpu.roll(a, LANES - shift, 1), b)
            arrays = swapped
            distance *= 2
        return arrays

    for c in range(channels_here):
        slot = c % SLOTS
        first = window_sum(2 * c)
        second = window_sum(2 * c + 1)
        scale = lax.rsqrt(second - first * first / length + 1e-05)
        framed_ref[slot, 0, :blocks, :] = records_ref[pl.ds(c, blocks, stride=pitch), :]
        here = framed_ref[slot, 0, :blocks, :]
        after = framed_ref[slot, 0, 1 : blocks + 1, :]
        for r in range(1, templ_here):
            turned = LANES - r * step
            framed_ref[slot, r, :blocks, :] = jnp.where(
                lane < turned, pltpu.roll(here, turned, 1), pltpu.roll(after, turned, 1)
            )
        frames = jnp.concatenate(
            [
                jnp.concatenate([framed_ref[slot, r, q : q + blocks, :].astype(bf16) for q in range(taps)], axis=1)
                for r in range(templ_here)
            ],
            axis=0,
        )
        product = jnp.dot(frames, weights_ref[c], preferred_element_type=f32)
        correlated = regroup([product[r * blocks : (r + 1) * blocks, :] for r in range(templ_here)], step)
        for t in range(templ_here):
            start = off_ref[t, c]
            down = start // LANES
            over = start % LANES
            moved_ref[slot, t, :blocks, :] = pltpu.roll(correlated[t] * scale, (LANES - over) % LANES, 1)
            near = moved_ref[slot, t, pl.ds(down, lag_blocks), :]
            far = moved_ref[slot, t, pl.ds(down + 1, lag_blocks), :]
            picked = jnp.where(lag_lane < LANES - over, near, far)
            weight = inv_ref[t, c : c + 1, :] * avail_ref[t, c].astype(f32)
            acc_ref[t, :lag_blocks, :] += picked * weight

    shares = out_ref.shape[0]
    own = lag_blocks // shares
    for t in range(templ_here):
        acc_ref[t, lag_blocks:, :] = acc_ref[t, :lag_blocks, :]
        for g in range(shares):
            out_ref[g, t * lag_blocks : (t + 1) * lag_blocks, :] = acc_ref[
                t, g * own : g * own + lag_blocks, :
            ].astype(out_ref.dtype)


def finish_kernel(parts_ref, out_ref):
    templ_here, share = out_ref.shape
    lag_blocks = parts_ref.shape[1] // templ_here
    for t in range(templ_here):
        rows = pl.ds(t * lag_blocks, lag_blocks)
        stack = parts_ref[0, rows, :].astype(jnp.float32)
        for g in range(1, parts_ref.shape[0]):
            stack = stack + parts_ref[g, rows, :].astype(jnp.float32)
        power = jnp.sum(jnp.sum(stack * stack, axis=0, keepdims=True), axis=1, keepdims=True)
        unit = 1.0 / jnp.sqrt(power / (lag_blocks * LANES) + 1e-05)
        for i in range(share // LANES):
            out_ref[t : t + 1, i * LANES : (i + 1) * LANES] = stack[i : i + 1, :] * unit


def spread_records(records, count):
    rows = padded_rows(records.shape[0])
    return pl.pallas_call(
        spread_kernel,
        out_shape=jax.ShapeDtypeStruct((count, rows, records.shape[1]), records.dtype),
        in_specs=[HBM],
        out_specs=HBM,
        scratch_shapes=[pltpu.SemaphoreType.DMA((count,))],
        compiler_params=limit(1),
        name="spread_records",
    )(records)


def prepared_weights(templates):
    templ_here, channels_here, length = templates.shape
    step = LANES // templ_here
    groups = -(-length // LANES)
    rows = padded_rows(channels_here)
    lines = pltpu.VMEM((groups, rows, templ_here * LANES), jnp.float32)
    chunks = pltpu.VMEM((groups * templ_here, rows, LANES), jnp.float32)
    return pl.pallas_call(
        weights_kernel,
        out_shape=(
            jax.ShapeDtypeStruct((channels_here, chunks_of(length, step) * step, LANES), jnp.bfloat16),
            jax.ShapeDtypeStruct((templ_here, channels_here, LANES), jnp.float32),
        ),
        in_specs=[VMEM],
        out_specs=(VMEM, VMEM),
        scratch_shapes=[lines, chunks],
        compiler_params=limit(16),
        name="prepare_weights",
    )(templates)


def partial_stacks(blocks, count, weights, inv, offsets, available, lag_count, length, shares):
    templ_here, channels_here, _ = inv.shape
    lag_blocks = lag_count // LANES
    total_rows = 2 * channels_here * count
    f32 = jnp.float32
    return pl.pallas_call(
        lambda *refs: stack_kernel(*refs, length=length),
        out_shape=jax.ShapeDtypeStruct((shares, templ_here * lag_blocks, LANES), jnp.bfloat16),
        in_specs=[HBM, HBM, VMEM, VMEM, VMEM],
        out_specs=VMEM,
        scratch_shapes=[
            pltpu.SMEM(offsets.shape, offsets.dtype),
            pltpu.SMEM(available.shape, available.dtype),
            pltpu.VMEM((total_rows, 3 * LANES), jnp.bfloat16),
            pltpu.VMEM((2 * channels_here, count + SUBLANES, 2 * LANES), f32),
            pltpu.VMEM((SLOTS, templ_here, count + SUBLANES, LANES), f32),
            pltpu.VMEM((SLOTS, templ_here, count + SUBLANES, LANES), f32),
            pltpu.VMEM((templ_here, 2 * lag_blocks, LANES), f32),
            pltpu.SemaphoreType.DMA((2,)),
        ],
        compiler_params=limit(24),
        name="stack_channels",
    )(offsets, available, blocks, weights, inv)


def finished(parts, templ_here, share):
    return pl.pallas_call(
        finish_kernel,
        out_shape=jax.ShapeDtypeStruct((templ_here, share), jnp.float32),
        in_specs=[VMEM],
        out_specs=VMEM,
        compiler_params=limit(4),
        name="finish",
    )(parts)


def shards(records, templates, offsets, available):
    block_len = records.shape[1]
    templ_here, _, length = templates.shape
    count = lax.axis_size("tmpl")
    shares = lax.axis_size("sta")
    lag_count = block_len * count - OFFMAX - length + 1
    blocks = lax.all_to_all(spread_records(records, count), "tmpl", 0, 0, tiled=True)
    weights, inv = prepared_weights(templates)
    parts = partial_stacks(
        blocks.reshape(-1, block_len), count, weights, inv, offsets, available, lag_count, length, shares
    )
    parts = lax.all_to_all(parts, "sta", 0, 0, tiled=True)
    return finished(parts, templ_here, lag_count // shares)


def solution(mesh):
    in_specs = (P("sta", "tmpl"), P("tmpl", "sta", None), P("tmpl", "sta"), P("tmpl", "sta"))
    out_specs = P("tmpl", "sta")
    return jax.shard_map(shards, mesh=mesh, in_specs=in_specs, out_specs=out_specs, check_vma=False)
```

```python
import jax
import jax.numpy as jnp
from jax import lax
from jax.experimental import pallas as pl
from jax.experimental.pallas import tpu as pltpu
from jax.sharding import PartitionSpec as P

OFFMAX = 425
LANES = 128
SUBLANES = 8
SLOTS = 4
SMEM = pl.BlockSpec(memory_space=pltpu.SMEM)
VMEM = pl.BlockSpec(memory_space=pltpu.VMEM)
HBM = pl.BlockSpec(memory_space=pltpu.HBM)


def padded_rows(rows):
    return -(-rows // SUBLANES) * SUBLANES


def chunks_of(length, step):
    return (length + 2 * step - 2) // step


def limit(mib):
    return pltpu.CompilerParams(vmem_limit_bytes=mib << 20)


def spread_kernel(records_ref, out_ref, tile_ref, sem):
    tile_ref[...] = jnp.zeros_like(tile_ref)
    tile_ref[: records_ref.shape[0], :] = records_ref[...]
    copies = [pltpu.make_async_copy(tile_ref, out_ref.at[i], sem.at[i]) for i in range(out_ref.shape[0])]
    for copy in copies:
        copy.start()
    for copy in copies:
        copy.wait()


def weights_kernel(templates_ref, weights_ref, inv_hbm, inv_ref, lines_ref, chunks_ref, sem):
    templ_here, channels_here, length = templates_ref.shape
    step = LANES // templ_here
    chunks = weights_ref.shape[1] // step
    groups = lines_ref.shape[0]
    width = templ_here * LANES
    bf16, f32 = jnp.bfloat16, jnp.float32
    lines_ref[...] = jnp.zeros_like(lines_ref)
    for t in range(templ_here):
        shapes = templates_ref[t]
        centred = shapes - jnp.sum(shapes, axis=1, keepdims=True) / length
        energy = jnp.sum(centred * centred, axis=1, keepdims=True)
        inv_ref[:, t * step : (t + 1) * step] = jnp.broadcast_to(lax.rsqrt(energy + 1e-05), (channels_here, step))
        for q in range(groups):
            here = min(LANES, length - q * LANES)
            lines_ref[q, :channels_here, t * LANES : t * LANES + here] = centred[:, q * LANES : q * LANES + here]
    inv_out = pltpu.make_async_copy(inv_ref, inv_hbm, sem)
    inv_out.start()
    col = lax.broadcasted_iota(jnp.int32, (1, width), 1)
    source = LANES * ((col % LANES) // step) + step * (col // LANES) + step - 1 - col % step
    pick = (lax.broadcasted_iota(jnp.int32, (width, width), 0) == source).astype(f32).astype(bf16)
    lines = lines_ref[...].reshape(groups * lines_ref.shape[1], width).astype(bf16)
    picked = jnp.dot(lines, pick, preferred_element_type=f32)
    rows = lines_ref.shape[1]
    for m in range(chunks_ref.shape[0]):
        q, i = divmod(m, templ_here)
        chunks_ref[m] = picked[q * rows : (q + 1) * rows, i * LANES : (i + 1) * LANES]

    row = lax.broadcasted_iota(jnp.int32, (step, LANES), 0)
    inside = lax.broadcasted_iota(jnp.int32, (step, LANES), 1) % step <= row

    for c in range(channels_here):
        before = jnp.zeros((step, LANES), f32)
        for m in range(chunks):
            if m * step < length:
                line = jnp.broadcast_to(chunks_ref[m, c : c + 1, :], (step, LANES))
                here = pltpu.roll(line, LANES - step + 1, 1, stride=1, stride_axis=0)
                following = pltpu.roll(line, 1, 1, stride=1, stride_axis=0)
            else:
                here = following = jnp.zeros((step, LANES), f32)
            weights_ref[c, m * step : (m + 1) * step, :] = jnp.where(inside, here, before).astype(bf16)
            before = following
    inv_out.wait()


def stack_kernel(
    off_hbm, avail_hbm, inv_hbm, records_ref, weights_ref, out_ref,
    off_ref, avail_ref, inv_ref, pieces_ref, tails_ref, totals_ref, acc_ref, sem, *slots,
    length,
):
    templ_here, channels_here = off_ref.shape
    step = LANES // templ_here
    blocks = tails_ref.shape[1] - SUBLANES
    framed = slots[: len(slots) // 2]
    moved = slots[len(slots) // 2 :]
    pitch = records_ref.shape[0] // blocks
    lag_blocks = acc_ref.shape[1]
    taps = weights_ref.shape[1] // LANES
    bf16, f32 = jnp.bfloat16, jnp.float32
    pairs = [(off_hbm, off_ref), (avail_hbm, avail_ref), (inv_hbm, inv_ref)]
    small = [pltpu.make_async_copy(*pair, sem.at[i]) for i, pair in enumerate(pairs)]
    for copy in small:
        copy.start()

    for c in range(channels_here):
        x = records_ref[pl.ds(c, blocks, stride=pitch), :]
        for k, v in enumerate((x, x * x)):
            rows = pl.ds((2 * c + k) * blocks, blocks)
            high = v.astype(bf16)
            rest = v - high.astype(f32)
            mid = rest.astype(bf16)
            low = (rest - mid.astype(f32)).astype(bf16)
            pieces_ref[rows, 0:LANES] = high
            pieces_ref[rows, LANES : 2 * LANES] = mid
            pieces_ref[rows, 2 * LANES : 3 * LANES] = low
    row = lax.broadcasted_iota(jnp.int32, (LANES, LANES), 0)
    col = lax.broadcasted_iota(jnp.int32, (LANES, LANES), 1)
    tail = (row >= col).astype(f32)
    adder = jnp.concatenate([tail, jnp.ones_like(tail)], axis=1).astype(bf16)
    adder = jnp.concatenate([adder, adder, adder], axis=0)
    sums = jnp.dot(pieces_ref[...], adder, preferred_element_type=f32)
    for k, ref in enumerate((tails_ref, totals_ref)):
        ref[:, :blocks, :] = sums[:, k * LANES : (k + 1) * LANES].reshape(2 * channels_here, blocks, LANES)
        ref[:, blocks:, :] = jnp.zeros((2 * channels_here, SUBLANES, LANES), f32)
    acc_ref[...] = jnp.zeros_like(acc_ref)
    for ref in framed:
        ref[blocks:, :] = jnp.zeros((SUBLANES, LANES), f32)
    for copy in small:
        copy.wait()

    whole = length // LANES
    turn = LANES - length % LANES
    lane = lax.broadcasted_iota(jnp.int32, (blocks, LANES), 1)
    lag_lane = lax.broadcasted_iota(jnp.int32, (lag_blocks, LANES), 1)

    def window_sum(index):
        def at(ref, i):
            return ref[index, i : i + blocks, :]

        total = at(tails_ref, 0)
        for i in range(1, whole + 1):
            total = total + at(totals_ref, i)
        ends = jnp.where(lane < turn, 0.0, at(totals_ref, whole + 1))
        near = pltpu.roll(at(tails_ref, whole), turn, 1)
        far = pltpu.roll(at(tails_ref, whole + 1), turn, 1)
        return total + (ends - jnp.where(lane < turn, near, far))

    def regroup(arrays, group):
        count = len(arrays)
        distance = 1
        while distance < count:
            kept = (lane // group) // distance % 2 == 0
            swapped = list(arrays)
            for r in range(count):
                if r // distance % 2 == 0:
                    a, b = arrays[r], arrays[r + distance]
                    shift = group * distance
                    swapped[r] = jnp.where(kept, a, pltpu.roll(b, shift, 1))
                    swapped[r + distance] = jnp.where(kept, pltpu.roll(a, LANES - shift, 1), b)
            arrays = swapped
            distance *= 2
        return arrays

    for c in range(channels_here):
        slot = c % SLOTS * templ_here
        first = window_sum(2 * c)
        second = window_sum(2 * c + 1)
        scale = lax.rsqrt(second - first * first / length + 1e-05)
        here = records_ref[pl.ds(c, blocks, stride=pitch), :]
        framed[slot][:blocks, :] = here
        for r in range(1, templ_here):
            ref = framed[slot + r]
            turned = pltpu.roll(here, LANES - r * step, 1)
            ref[:blocks, :] = turned
            ref[:blocks, :] = jnp.where(lane < LANES - r * step, turned, ref[1 : blocks + 1, :])
        frames = jnp.concatenate(
            [
                jnp.concatenate([framed[slot + r][q : q + blocks, :].astype(bf16) for q in range(taps)], axis=1)
                for r in range(templ_here)
            ],
            axis=0,
        )
        product = jnp.dot(frames, weights_ref[c], preferred_element_type=f32) * inv_ref[c : c + 1, :]
        correlated = regroup([product[r * blocks : (r + 1) * blocks, :] for r in range(templ_here)], step)
        for t in range(templ_here):
            start = off_ref[t, c]
            down = start // LANES
            over = start % LANES
            ref = moved[slot + t]
            ref[:blocks, :] = pltpu.roll(correlated[t] * scale, (LANES - over) % LANES, 1)
            near = ref[pl.ds(down, lag_blocks), :]
            far = ref[pl.ds(down + 1, lag_blocks), :]
            picked = jnp.where(lag_lane < LANES - over, near, far)
            acc_ref[t] += picked * avail_ref[t, c].astype(f32)

    for t in range(templ_here):
        out_ref[t * lag_blocks : (t + 1) * lag_blocks, :] = acc_ref[t]


def finish_kernel(place_ref, *refs):
    *parts, out_ref, stack_ref = refs
    templ_here, share = out_ref.shape
    lag_blocks = stack_ref.shape[0] // templ_here
    own = share // LANES
    for t in range(templ_here):
        rows = pl.ds(t * lag_blocks, lag_blocks)
        stack = parts[0][rows, :].astype(jnp.float32)
        for part in parts[1:]:
            stack = stack + part[rows, :].astype(jnp.float32)
        stack_ref[rows, :] = stack
        power = jnp.sum(jnp.sum(stack * stack, axis=0, keepdims=True), axis=1, keepdims=True)
        unit = 1.0 / jnp.sqrt(power / (lag_blocks * LANES) + 1e-05)
        for i in range(own):
            line = stack_ref[pl.ds(t * lag_blocks + place_ref[0] * own + i, 1), :]
            out_ref[t : t + 1, i * LANES : (i + 1) * LANES] = line * unit


def spread_records(records, count):
    rows = padded_rows(records.shape[0])
    return pl.pallas_call(
        spread_kernel,
        out_shape=jax.ShapeDtypeStruct((count, rows, records.shape[1]), records.dtype),
        in_specs=[VMEM],
        out_specs=HBM,
        scratch_shapes=[pltpu.VMEM((rows, records.shape[1]), records.dtype), pltpu.SemaphoreType.DMA((count,))],
        compiler_params=limit(1),
        name="spread_records",
    )(records)


def prepared_weights(templates):
    templ_here, channels_here, length = templates.shape
    step = LANES // templ_here
    groups = -(-length // LANES)
    rows = padded_rows(channels_here)
    lines = pltpu.VMEM((groups, rows, templ_here * LANES), jnp.float32)
    chunks = pltpu.VMEM((groups * templ_here, rows, LANES), jnp.float32)
    return pl.pallas_call(
        weights_kernel,
        out_shape=(
            jax.ShapeDtypeStruct((channels_here, chunks_of(length, step) * step, LANES), jnp.bfloat16),
            pltpu.HBM((channels_here, LANES), jnp.float32),
        ),
        in_specs=[VMEM],
        out_specs=(VMEM, HBM),
        scratch_shapes=[pltpu.VMEM((channels_here, LANES), jnp.float32), lines, chunks, pltpu.SemaphoreType.DMA(())],
        compiler_params=limit(16),
        name="prepare_weights",
    )(templates)


def partial_stacks(blocks, count, weights, inv, offsets, available, lag_count, length):
    templ_here, channels_here = offsets.shape
    offsets, available, inv = (pltpu.with_memory_space_constraint(a, pltpu.HBM) for a in (offsets, available, inv))
    lag_blocks = lag_count // LANES
    total_rows = 2 * channels_here * count
    f32 = jnp.float32
    return pl.pallas_call(
        lambda *refs: stack_kernel(*refs, length=length),
        out_shape=jax.ShapeDtypeStruct((templ_here * lag_blocks, LANES), f32),
        in_specs=[HBM, HBM, HBM, VMEM, VMEM],
        out_specs=VMEM,
        scratch_shapes=[
            pltpu.SMEM(offsets.shape, offsets.dtype),
            pltpu.SMEM(available.shape, available.dtype),
            pltpu.VMEM(inv.shape, f32),
            pltpu.VMEM((total_rows, 3 * LANES), jnp.bfloat16),
            pltpu.VMEM((2 * channels_here, count + SUBLANES, LANES), f32),
            pltpu.VMEM((2 * channels_here, count + SUBLANES, LANES), f32),
            pltpu.VMEM((templ_here, lag_blocks, LANES), f32),
            pltpu.SemaphoreType.DMA((3,)),
        ]
        + [pltpu.VMEM((count + SUBLANES, LANES), f32)] * (2 * SLOTS * templ_here),
        compiler_params=limit(24),
        name="stack_channels",
    )(offsets, available, inv, blocks, weights)


def finished(place, parts, templ_here, share):
    return pl.pallas_call(
        finish_kernel,
        out_shape=jax.ShapeDtypeStruct((templ_here, share), jnp.float32),
        in_specs=[SMEM] + [VMEM] * len(parts),
        out_specs=VMEM,
        scratch_shapes=[pltpu.VMEM(parts[0].shape, jnp.float32)],
        compiler_params=limit(4),
        name="finish",
    )(place, *parts)


MODE = "near_first"


def swapped(array, distance):
    return lax.ppermute(array, "sta", [(i, i ^ distance) for i in range(lax.axis_size("sta"))])


def shards(records, templates, offsets, available):
    block_len = records.shape[1]
    templ_here, _, length = templates.shape
    count = lax.axis_size("tmpl")
    shares = lax.axis_size("sta")
    lag_count = block_len * count - OFFMAX - length + 1
    blocks = lax.all_to_all(spread_records(records, count), "tmpl", 0, 0, tiled=True)
    weights, inv = prepared_weights(templates)
    mine = partial_stacks(blocks.reshape(-1, block_len), count, weights, inv, offsets, available, lag_count, length)
    place = lax.axis_index("sta").reshape(1).astype(jnp.int32)
    bf16 = jnp.bfloat16
    if MODE == "doubling":
        two = mine + swapped(mine, 1)
        four = two + swapped(two.astype(bf16), 2).astype(jnp.float32)
        parts = [four, swapped(four.astype(bf16), 4)]
    elif MODE == "core_last":
        low = mine.astype(bf16)
        four = mine + sum(swapped(low, d).astype(jnp.float32) for d in (2, 6, 4))
        parts = [four, swapped(four, 1)]
    else:
        theirs = swapped(mine, 1)
        low = (mine + theirs).astype(bf16)
        order = {"near_first": (2, 6, 4), "far_first": (4, 2, 6)}[MODE]
        parts = [mine, theirs] + [swapped(low, d) for d in order]
    return finished(place, parts, templ_here, lag_count // shares)


def solution(mesh):
    in_specs = (P("sta", "tmpl"), P("tmpl", "sta", None), P("tmpl", "sta"), P("tmpl", "sta"))
    out_specs = P("tmpl", "sta")
    return jax.shard_map(shards, mesh=mesh, in_specs=in_specs, out_specs=out_specs, check_vma=False)
```

```python
import jax
import jax.numpy as jnp
from jax import lax
from jax.experimental import pallas as pl
from jax.experimental.pallas import tpu as pltpu
from jax.sharding import PartitionSpec as P

OFFMAX = 425
LANES = 128
SUBLANES = 8
SMEM = pl.BlockSpec(memory_space=pltpu.SMEM)
VMEM = pl.BlockSpec(memory_space=pltpu.VMEM)
HBM = pl.BlockSpec(memory_space=pltpu.HBM)


def padded_rows(rows):
    return -(-rows // SUBLANES) * SUBLANES


def chunks_of(length, step):
    return (length + 2 * step - 2) // step


def limit(mib):
    return pltpu.CompilerParams(vmem_limit_bytes=mib << 20)


def spread_kernel(records_ref, out_ref, tile_ref, sem):
    tile_ref[...] = jnp.zeros_like(tile_ref)
    tile_ref[: records_ref.shape[0], :] = records_ref[...]
    copies = [pltpu.make_async_copy(tile_ref, out_ref.at[i], sem.at[i]) for i in range(out_ref.shape[0])]
    for copy in copies:
        copy.start()
    for copy in copies:
        copy.wait()


def weights_kernel(templates_ref, weights_ref, inv_hbm, inv_ref, lines_ref, chunks_ref, sem):
    templ_here, channels_here, length = templates_ref.shape
    step = LANES // templ_here
    chunks = weights_ref.shape[1] // step
    groups = lines_ref.shape[0]
    width = templ_here * LANES
    bf16, f32 = jnp.bfloat16, jnp.float32
    lines_ref[...] = jnp.zeros_like(lines_ref)
    for t in range(templ_here):
        shapes = templates_ref[t]
        centred = shapes - jnp.sum(shapes, axis=1, keepdims=True) / length
        energy = jnp.sum(centred * centred, axis=1, keepdims=True)
        inv_ref[:, t * step : (t + 1) * step] = jnp.broadcast_to(lax.rsqrt(energy + 1e-05), (channels_here, step))
        for q in range(groups):
            here = min(LANES, length - q * LANES)
            lines_ref[q, :channels_here, t * LANES : t * LANES + here] = centred[:, q * LANES : q * LANES + here]
    inv_out = pltpu.make_async_copy(inv_ref, inv_hbm, sem)
    inv_out.start()
    col = lax.broadcasted_iota(jnp.int32, (1, width), 1)
    source = LANES * ((col % LANES) // step) + step * (col // LANES) + step - 1 - col % step
    pick = (lax.broadcasted_iota(jnp.int32, (width, width), 0) == source).astype(f32).astype(bf16)
    lines = lines_ref[...].reshape(groups * lines_ref.shape[1], width).astype(bf16)
    picked = jnp.dot(lines, pick, preferred_element_type=f32)
    rows = lines_ref.shape[1]
    for m in range(chunks_ref.shape[0]):
        q, i = divmod(m, templ_here)
        chunks_ref[m] = picked[q * rows : (q + 1) * rows, i * LANES : (i + 1) * LANES]

    row = lax.broadcasted_iota(jnp.int32, (step, LANES), 0)
    inside = lax.broadcasted_iota(jnp.int32, (step, LANES), 1) % step <= row

    for c in range(channels_here):
        before = jnp.zeros((step, LANES), f32)
        for m in range(chunks):
            if m * step < length:
                line = jnp.broadcast_to(chunks_ref[m, c : c + 1, :], (step, LANES))
                here = pltpu.roll(line, LANES - step + 1, 1, stride=1, stride_axis=0)
                following = pltpu.roll(line, 1, 1, stride=1, stride_axis=0)
            else:
                here = following = jnp.zeros((step, LANES), f32)
            weights_ref[c, m * step : (m + 1) * step, :] = jnp.where(inside, here, before).astype(bf16)
            before = following
    inv_out.wait()


def stack_kernel(
    off_hbm, avail_hbm, inv_hbm, records_ref, weights_ref, out_ref,
    off_ref, avail_ref, inv_ref, pieces_ref, tails_ref, totals_ref, heads_ref, sem, *slots,
    length,
):
    templ_here, channels_here = off_ref.shape
    step = LANES // templ_here
    blocks = tails_ref.shape[1] - SUBLANES
    framed = slots[: len(slots) // 2]
    moved = slots[len(slots) // 2 :]
    pitch = records_ref.shape[0] // blocks
    lag_blocks = out_ref.shape[0] // templ_here
    taps = weights_ref.shape[1] // LANES
    bf16, f32 = jnp.bfloat16, jnp.float32
    pairs = [(off_hbm, off_ref), (avail_hbm, avail_ref), (inv_hbm, inv_ref)]
    small = [pltpu.make_async_copy(*pair, sem.at[i]) for i, pair in enumerate(pairs)]
    for copy in small:
        copy.start()

    row = lax.broadcasted_iota(jnp.int32, (LANES, LANES), 0)
    col = lax.broadcasted_iota(jnp.int32, (LANES, LANES), 1)
    turn = LANES - length % LANES
    kinds = (row >= col, row >= 0, row < (col - turn) % LANES)
    adder = jnp.concatenate([kind.astype(f32) for kind in kinds], axis=1).astype(bf16)
    adder = jnp.concatenate([adder, adder], axis=0)

    def block_sums():
        for c in range(channels_here):
            x = records_ref[pl.ds(c, blocks, stride=pitch), :]
            for k, v in enumerate((x, x * x)):
                rows = pl.ds((2 * c + k) * blocks, blocks)
                high = v.astype(bf16)
                pieces_ref[rows, 0:LANES] = high
                pieces_ref[rows, LANES : 2 * LANES] = (v - high.astype(f32)).astype(bf16)
        sums = jnp.dot(pieces_ref[...], adder, preferred_element_type=f32)
        count = 2 * channels_here
        for k, ref in enumerate((tails_ref, totals_ref, heads_ref)):
            ref[:, :blocks, :] = sums[:, k * LANES : (k + 1) * LANES].reshape(count, blocks, LANES)
            ref[:, blocks:, :] = jnp.zeros((count, SUBLANES, LANES), f32)

    stacks = [jnp.zeros((lag_blocks, LANES), f32) for _ in range(templ_here)]
    for ref in framed:
        ref[blocks:, :] = jnp.zeros((SUBLANES, LANES), f32)
    for copy in small:
        copy.wait()

    whole = length // LANES
    lane = lax.broadcasted_iota(jnp.int32, (blocks, LANES), 1)
    lag_lane = lax.broadcasted_iota(jnp.int32, (lag_blocks, LANES), 1)

    def window_sum(index):
        def at(ref, i):
            return ref[index, i : i + blocks, :]

        total = at(tails_ref, 0)
        for i in range(1, whole):
            total = total + at(totals_ref, i)
        ends = jnp.where(lane < turn, at(heads_ref, whole), at(totals_ref, whole) + at(heads_ref, whole + 1))
        return total + ends

    def regroup(arrays, group):
        count = len(arrays)
        distance = 1
        while distance < count:
            kept = (lane // group) // distance % 2 == 0
            swapped = list(arrays)
            for r in range(count):
                if r // distance % 2 == 0:
                    a, b = arrays[r], arrays[r + distance]
                    shift = group * distance
                    swapped[r] = jnp.where(kept, a, pltpu.roll(b, shift, 1))
                    swapped[r + distance] = jnp.where(kept, pltpu.roll(a, LANES - shift, 1), b)
            arrays = swapped
            distance *= 2
        return arrays

    block_sums()
    for c in range(channels_here):
        slot = c * templ_here
        first = window_sum(2 * c)
        second = window_sum(2 * c + 1)
        scale = lax.rsqrt(second - first * first / length + 1e-05)
        here = records_ref[pl.ds(c, blocks, stride=pitch), :]
        framed[slot][:blocks, :] = here
        for r in range(1, templ_here):
            ref = framed[slot + r]
            turned = pltpu.roll(here, LANES - r * step, 1)
            ref[:blocks, :] = turned
            ref[:blocks, :] = jnp.where(lane < LANES - r * step, turned, ref[1 : blocks + 1, :])
        frames = jnp.concatenate(
            [
                jnp.concatenate([framed[slot + r][q : q + blocks, :].astype(bf16) for q in range(taps)], axis=1)
                for r in range(templ_here)
            ],
            axis=0,
        )
        product = jnp.dot(frames, weights_ref[c], preferred_element_type=f32) * inv_ref[c : c + 1, :]
        correlated = regroup([product[r * blocks : (r + 1) * blocks, :] for r in range(templ_here)], step)
        for t in range(templ_here):
            start = off_ref[t, c]
            down = start // LANES
            over = start % LANES
            ref = moved[slot + t]
            ref[:blocks, :] = pltpu.roll(correlated[t] * scale, (LANES - over) % LANES, 1)
            near = ref[pl.ds(down, lag_blocks), :]
            far = ref[pl.ds(down + 1, lag_blocks), :]
            picked = jnp.where(lag_lane < LANES - over, near, far)
            stacks[t] = stacks[t] + picked * avail_ref[t, c].astype(f32)

    for t in range(templ_here):
        out_ref[t * lag_blocks : (t + 1) * lag_blocks, :] = stacks[t]


def finish_kernel(place_ref, *refs):
    *parts, out_ref, stack_ref = refs
    templ_here, share = out_ref.shape
    lag_blocks = stack_ref.shape[0] // templ_here
    own = share // LANES
    for t in range(templ_here):
        rows = pl.ds(t * lag_blocks, lag_blocks)
        stack = parts[0][rows, :].astype(jnp.float32)
        for part in parts[1:]:
            stack = stack + part[rows, :].astype(jnp.float32)
        stack_ref[rows, :] = stack
        power = jnp.sum(jnp.sum(stack * stack, axis=0, keepdims=True), axis=1, keepdims=True)
        unit = 1.0 / jnp.sqrt(power / (lag_blocks * LANES) + 1e-05)
        for i in range(own):
            line = stack_ref[pl.ds(t * lag_blocks + place_ref[0] * own + i, 1), :]
            out_ref[t : t + 1, i * LANES : (i + 1) * LANES] = line * unit


def spread_records(records, count):
    rows = padded_rows(records.shape[0])
    return pl.pallas_call(
        spread_kernel,
        out_shape=jax.ShapeDtypeStruct((count, rows, records.shape[1]), records.dtype),
        in_specs=[VMEM],
        out_specs=HBM,
        scratch_shapes=[pltpu.VMEM((rows, records.shape[1]), records.dtype), pltpu.SemaphoreType.DMA((count,))],
        compiler_params=limit(1),
        name="spread_records",
    )(records)


def prepared_weights(templates):
    templ_here, channels_here, length = templates.shape
    step = LANES // templ_here
    groups = -(-length // LANES)
    rows = padded_rows(channels_here)
    lines = pltpu.VMEM((groups, rows, templ_here * LANES), jnp.float32)
    chunks = pltpu.VMEM((groups * templ_here, rows, LANES), jnp.float32)
    return pl.pallas_call(
        weights_kernel,
        out_shape=(
            jax.ShapeDtypeStruct((channels_here, chunks_of(length, step) * step, LANES), jnp.bfloat16),
            pltpu.HBM((channels_here, LANES), jnp.float32),
        ),
        in_specs=[VMEM],
        out_specs=(VMEM, HBM),
        scratch_shapes=[pltpu.VMEM((channels_here, LANES), jnp.float32), lines, chunks, pltpu.SemaphoreType.DMA(())],
        compiler_params=limit(16),
        name="prepare_weights",
    )(templates)


def partial_stacks(blocks, count, weights, inv, offsets, available, lag_count, length):
    templ_here, channels_here = offsets.shape
    offsets, available, inv = (pltpu.with_memory_space_constraint(a, pltpu.HBM) for a in (offsets, available, inv))
    lag_blocks = lag_count // LANES
    total_rows = 2 * channels_here * count
    f32 = jnp.float32
    return pl.pallas_call(
        lambda *refs: stack_kernel(*refs, length=length),
        out_shape=jax.ShapeDtypeStruct((templ_here * lag_blocks, LANES), f32),
        in_specs=[HBM, HBM, HBM, VMEM, VMEM],
        out_specs=VMEM,
        scratch_shapes=[
            pltpu.SMEM(offsets.shape, offsets.dtype),
            pltpu.SMEM(available.shape, available.dtype),
            pltpu.VMEM(inv.shape, f32),
            pltpu.VMEM((total_rows, 2 * LANES), jnp.bfloat16),
            pltpu.VMEM((2 * channels_here, count + SUBLANES, LANES), f32),
            pltpu.VMEM((2 * channels_here, count + SUBLANES, LANES), f32),
            pltpu.VMEM((2 * channels_here, count + SUBLANES, LANES), f32),
            pltpu.SemaphoreType.DMA((3,)),
        ]
        + [pltpu.VMEM((count + SUBLANES, LANES), f32)] * (2 * channels_here * templ_here),
        compiler_params=limit(24),
        name="stack_channels",
    )(offsets, available, inv, blocks, weights)


def finished(place, parts, templ_here, share):
    return pl.pallas_call(
        finish_kernel,
        out_shape=jax.ShapeDtypeStruct((templ_here, share), jnp.float32),
        in_specs=[SMEM] + [VMEM] * len(parts),
        out_specs=VMEM,
        scratch_shapes=[pltpu.VMEM(parts[0].shape, jnp.float32)],
        compiler_params=limit(4),
        name="finish",
    )(place, *parts)


def swapped(array, distance):
    return lax.ppermute(array, "sta", [(i, i ^ distance) for i in range(lax.axis_size("sta"))])


def shards(records, templates, offsets, available):
    block_len = records.shape[1]
    templ_here, _, length = templates.shape
    count = lax.axis_size("tmpl")
    shares = lax.axis_size("sta")
    lag_count = block_len * count - OFFMAX - length + 1
    blocks = lax.all_to_all(spread_records(records, count), "tmpl", 0, 0, tiled=True)
    weights, inv = prepared_weights(templates)
    mine = partial_stacks(blocks.reshape(-1, block_len), count, weights, inv, offsets, available, lag_count, length)
    place = lax.axis_index("sta").reshape(1).astype(jnp.int32)
    theirs = swapped(mine, 1)
    pair = (mine + theirs).astype(jnp.bfloat16)
    parts = [mine, theirs] + [swapped(pair, distance) for distance in (2, 6, 4)]
    return finished(place, parts, templ_here, lag_count // shares)


def solution(mesh):
    in_specs = (P("sta", "tmpl"), P("tmpl", "sta", None), P("tmpl", "sta"), P("tmpl", "sta"))
    out_specs = P("tmpl", "sta")
    return jax.shard_map(shards, mesh=mesh, in_specs=in_specs, out_specs=out_specs, check_vma=False)
```

```python
import jax
import jax.numpy as jnp
from jax import lax
from jax.experimental import pallas as pl
from jax.experimental.pallas import tpu as pltpu
from jax.sharding import PartitionSpec as P

OFFMAX = 425
LANES = 128
SUBLANES = 8
SMEM = pl.BlockSpec(memory_space=pltpu.SMEM)
VMEM = pl.BlockSpec(memory_space=pltpu.VMEM)
HBM = pl.BlockSpec(memory_space=pltpu.HBM)


def padded_rows(rows):
    return -(-rows // SUBLANES) * SUBLANES


def chunks_of(length, step):
    return (length + 2 * step - 2) // step


def limit(mib):
    return pltpu.CompilerParams(vmem_limit_bytes=mib << 20)


def weights_kernel(
    off_hbm, avail_hbm, templates_ref, weights_ref, inv_ref, coded_ref, off_ref, avail_ref, lines_ref, chunks_ref, sem
):
    templ_here, channels_here, length = templates_ref.shape
    step = LANES // templ_here
    chunks = weights_ref.shape[1] // step
    groups = lines_ref.shape[0]
    width = templ_here * LANES
    bf16, f32 = jnp.bfloat16, jnp.float32
    small = [
        pltpu.make_async_copy(off_hbm, off_ref, sem.at[0]),
        pltpu.make_async_copy(avail_hbm, avail_ref, sem.at[1]),
    ]
    for copy in small:
        copy.start()
    lines_ref[...] = jnp.zeros_like(lines_ref)
    for t in range(templ_here):
        shapes = templates_ref[t]
        centred = shapes - jnp.sum(shapes, axis=1, keepdims=True) / length
        energy = jnp.sum(centred * centred, axis=1, keepdims=True)
        inv_ref[:, t * step : (t + 1) * step] = jnp.broadcast_to(lax.rsqrt(energy + 1e-05), (channels_here, step))
        for q in range(groups):
            here = min(LANES, length - q * LANES)
            lines_ref[q, :channels_here, t * LANES : t * LANES + here] = centred[:, q * LANES : q * LANES + here]
    col = lax.broadcasted_iota(jnp.int32, (1, width), 1)
    source = LANES * ((col % LANES) // step) + step * (col // LANES) + step - 1 - col % step
    pick = (lax.broadcasted_iota(jnp.int32, (width, width), 0) == source).astype(f32).astype(bf16)
    lines = lines_ref[...].reshape(groups * lines_ref.shape[1], width).astype(bf16)
    picked = jnp.dot(lines, pick, preferred_element_type=f32)
    rows = lines_ref.shape[1]
    for m in range(chunks_ref.shape[0]):
        q, i = divmod(m, templ_here)
        chunks_ref[m] = picked[q * rows : (q + 1) * rows, i * LANES : (i + 1) * LANES]

    row = lax.broadcasted_iota(jnp.int32, (step, LANES), 0)
    inside = lax.broadcasted_iota(jnp.int32, (step, LANES), 1) % step <= row

    for c in range(channels_here):
        before = jnp.zeros((step, LANES), f32)
        for m in range(chunks):
            if m * step < length:
                line = jnp.broadcast_to(chunks_ref[m, c : c + 1, :], (step, LANES))
                here = pltpu.roll(line, LANES - step + 1, 1, stride=1, stride_axis=0)
                following = pltpu.roll(line, 1, 1, stride=1, stride_axis=0)
            else:
                here = following = jnp.zeros((step, LANES), f32)
            weights_ref[c, m * step : (m + 1) * step, :] = jnp.where(inside, here, before).astype(bf16)
            before = following
    for copy in small:
        copy.wait()
    coded_ref[...] = 2 * off_ref[...] + avail_ref[...]


def stack_kernel(
    coded_ref, inv_ref, records_ref, weights_ref, out_ref,
    picks_ref, pieces_ref, tails_ref, totals_ref, heads_ref, sem, *slots,
    length,
):
    templ_here, channels_here = coded_ref.shape
    step = LANES // templ_here
    blocks = tails_ref.shape[1] - SUBLANES
    framed = slots[: len(slots) // 2]
    moved = slots[len(slots) // 2 :]
    pitch = records_ref.shape[0] // blocks
    lag_blocks = out_ref.shape[0] // templ_here
    taps = weights_ref.shape[1] // LANES
    bf16, f32 = jnp.bfloat16, jnp.float32
    picks = pltpu.make_async_copy(coded_ref, picks_ref, sem)
    picks.start()
    row = lax.broadcasted_iota(jnp.int32, (LANES, LANES), 0)
    col = lax.broadcasted_iota(jnp.int32, (LANES, LANES), 1)
    turn = LANES - length % LANES
    kinds = (row >= col, row >= 0, row < (col - turn) % LANES)
    adder = jnp.concatenate([kind.astype(f32) for kind in kinds], axis=1).astype(bf16)
    adder = jnp.concatenate([adder, adder], axis=0)

    def block_sums():
        for c in range(channels_here):
            x = records_ref[pl.ds(c, blocks, stride=pitch), :]
            for k, v in enumerate((x, x * x)):
                rows = pl.ds((2 * c + k) * blocks, blocks)
                high = v.astype(bf16)
                pieces_ref[rows, 0:LANES] = high
                pieces_ref[rows, LANES : 2 * LANES] = (v - high.astype(f32)).astype(bf16)
        picks.wait()
        sums = jnp.dot(pieces_ref[...], adder, preferred_element_type=f32)
        count = 2 * channels_here
        for k, ref in enumerate((tails_ref, totals_ref, heads_ref)):
            ref[:, :blocks, :] = sums[:, k * LANES : (k + 1) * LANES].reshape(count, blocks, LANES)
            ref[:, blocks:, :] = jnp.zeros((count, SUBLANES, LANES), f32)

    stacks = [jnp.zeros((lag_blocks, LANES), f32) for _ in range(templ_here)]
    for ref in framed:
        ref[blocks:, :] = jnp.zeros((SUBLANES, LANES), f32)

    whole = length // LANES
    lane = lax.broadcasted_iota(jnp.int32, (blocks, LANES), 1)
    lag_lane = lax.broadcasted_iota(jnp.int32, (lag_blocks, LANES), 1)

    def window_sum(index):
        def at(ref, i):
            return ref[index, i : i + blocks, :]

        total = at(tails_ref, 0)
        for i in range(1, whole):
            total = total + at(totals_ref, i)
        ends = jnp.where(lane < turn, at(heads_ref, whole), at(totals_ref, whole) + at(heads_ref, whole + 1))
        return total + ends

    def regroup(arrays, group):
        count = len(arrays)
        distance = 1
        while distance < count:
            kept = (lane // group) // distance % 2 == 0
            swapped = list(arrays)
            for r in range(count):
                if r // distance % 2 == 0:
                    a, b = arrays[r], arrays[r + distance]
                    shift = group * distance
                    swapped[r] = jnp.where(kept, a, pltpu.roll(b, shift, 1))
                    swapped[r + distance] = jnp.where(kept, pltpu.roll(a, LANES - shift, 1), b)
            arrays = swapped
            distance *= 2
        return arrays

    block_sums()
    for c in range(channels_here):
        slot = c * templ_here
        first = window_sum(2 * c)
        second = window_sum(2 * c + 1)
        scale = lax.rsqrt(second - first * first / length + 1e-05)
        here = records_ref[pl.ds(c, blocks, stride=pitch), :]
        framed[slot][:blocks, :] = here
        for r in range(1, templ_here):
            ref = framed[slot + r]
            turned = pltpu.roll(here, LANES - r * step, 1)
            ref[:blocks, :] = turned
            ref[:blocks, :] = jnp.where(lane < LANES - r * step, turned, ref[1 : blocks + 1, :])
        frames = jnp.concatenate(
            [
                jnp.concatenate([framed[slot + r][q : q + blocks, :].astype(bf16) for q in range(taps)], axis=1)
                for r in range(templ_here)
            ],
            axis=0,
        )
        product = jnp.dot(frames, weights_ref[c], preferred_element_type=f32) * inv_ref[c : c + 1, :]
        correlated = regroup([product[r * blocks : (r + 1) * blocks, :] for r in range(templ_here)], step)
        for t in range(templ_here):
            pick = picks_ref[t, c]
            down = pick // (2 * LANES)
            over = pick // 2 % LANES
            ref = moved[slot + t]
            ref[:blocks, :] = pltpu.roll(correlated[t] * scale, (LANES - over) % LANES, 1)
            near = ref[pl.ds(down, lag_blocks), :]
            far = ref[pl.ds(down + 1, lag_blocks), :]
            picked = jnp.where(lag_lane < LANES - over, near, far)
            stacks[t] = stacks[t] + picked * (pick % 2).astype(f32)

    for t in range(templ_here):
        out_ref[t * lag_blocks : (t + 1) * lag_blocks, :] = stacks[t]


def finish_kernel(place_ref, *refs):
    *parts, out_ref, stack_ref = refs
    templ_here, share = out_ref.shape
    lag_blocks = stack_ref.shape[0] // templ_here
    own = share // LANES
    for t in range(templ_here):
        rows = pl.ds(t * lag_blocks, lag_blocks)
        stack = parts[0][rows, :].astype(jnp.float32)
        for part in parts[1:]:
            stack = stack + part[rows, :].astype(jnp.float32)
        stack_ref[rows, :] = stack
        power = jnp.sum(jnp.sum(stack * stack, axis=0, keepdims=True), axis=1, keepdims=True)
        unit = 1.0 / jnp.sqrt(power / (lag_blocks * LANES) + 1e-05)
        for i in range(own):
            line = stack_ref[pl.ds(t * lag_blocks + place_ref[0] * own + i, 1), :]
            out_ref[t : t + 1, i * LANES : (i + 1) * LANES] = line * unit


def spread_records(records, count):
    channels_here, block_len = records.shape
    return jnp.broadcast_to(records.reshape(1, channels_here, 1, block_len), (count, channels_here, 1, block_len))


def prepared_weights(templates, offsets, available):
    templ_here, channels_here, length = templates.shape
    step = LANES // templ_here
    groups = -(-length // LANES)
    rows = padded_rows(channels_here)
    lines = pltpu.VMEM((groups, rows, templ_here * LANES), jnp.float32)
    chunks = pltpu.VMEM((groups * templ_here, rows, LANES), jnp.float32)
    return pl.pallas_call(
        weights_kernel,
        out_shape=(
            jax.ShapeDtypeStruct((channels_here, chunks_of(length, step) * step, LANES), jnp.bfloat16),
            jax.ShapeDtypeStruct((channels_here, LANES), jnp.float32),
            jax.ShapeDtypeStruct(offsets.shape, jnp.int32),
        ),
        in_specs=[HBM, HBM, VMEM],
        out_specs=(VMEM, VMEM, VMEM),
        scratch_shapes=[
            pltpu.VMEM(offsets.shape, jnp.int32),
            pltpu.VMEM(offsets.shape, jnp.int32),
            lines,
            chunks,
            pltpu.SemaphoreType.DMA((2,)),
        ],
        compiler_params=limit(16),
        name="prepare_weights",
    )(*(pltpu.with_memory_space_constraint(a, pltpu.HBM) for a in (offsets, available)), templates)


def partial_stacks(blocks, count, weights, inv, coded, lag_count, length):
    templ_here, channels_here = coded.shape
    lag_blocks = lag_count // LANES
    total_rows = 2 * channels_here * count
    f32 = jnp.float32
    return pl.pallas_call(
        lambda *refs: stack_kernel(*refs, length=length),
        out_shape=jax.ShapeDtypeStruct((templ_here * lag_blocks, LANES), f32),
        in_specs=[VMEM, VMEM, VMEM, VMEM],
        out_specs=VMEM,
        scratch_shapes=[
            pltpu.SMEM(coded.shape, coded.dtype),
            pltpu.VMEM((total_rows, 2 * LANES), jnp.bfloat16),
            pltpu.VMEM((2 * channels_here, count + SUBLANES, LANES), f32),
            pltpu.VMEM((2 * channels_here, count + SUBLANES, LANES), f32),
            pltpu.VMEM((2 * channels_here, count + SUBLANES, LANES), f32),
            pltpu.SemaphoreType.DMA(()),
        ]
        + [pltpu.VMEM((count + SUBLANES, LANES), f32)] * (2 * channels_here * templ_here),
        compiler_params=limit(24),
        name="stack_channels",
    )(coded, inv, blocks, weights)


def finished(place, parts, templ_here, share):
    return pl.pallas_call(
        finish_kernel,
        out_shape=jax.ShapeDtypeStruct((templ_here, share), jnp.float32),
        in_specs=[SMEM] + [VMEM] * len(parts),
        out_specs=VMEM,
        scratch_shapes=[pltpu.VMEM(parts[0].shape, jnp.float32)],
        compiler_params=limit(4),
        name="finish",
    )(place, *parts)


ORDER = (1, 2, 6)


def swapped(array, distance):
    return lax.ppermute(array, "sta", [(i, i ^ distance) for i in range(lax.axis_size("sta"))])


def shards(records, templates, offsets, available):
    block_len = records.shape[1]
    templ_here, _, length = templates.shape
    count = lax.axis_size("tmpl")
    shares = lax.axis_size("sta")
    lag_count = block_len * count - OFFMAX - length + 1
    blocks = lax.all_to_all(spread_records(records, count), "tmpl", 0, 0, tiled=True)
    weights, inv, coded = prepared_weights(templates, offsets, available)
    mine = partial_stacks(blocks.reshape(-1, block_len), count, weights, inv, coded, lag_count, length)
    place = lax.axis_index("sta").reshape(1).astype(jnp.int32)
    bf16, f32 = jnp.bfloat16, jnp.float32
    parts = [mine]
    for distance in ORDER:
        mine = parts[0] if len(parts) == 1 else parts[0] + parts[1].astype(f32)
        parts = [mine, swapped(mine if distance == 1 else mine.astype(bf16), distance)]
    return finished(place, parts, templ_here, lag_count // shares)


def solution(mesh):
    in_specs = (P("sta", "tmpl"), P("tmpl", "sta", None), P("tmpl", "sta"), P("tmpl", "sta"))
    out_specs = P("tmpl", "sta")
    return jax.shard_map(shards, mesh=mesh, in_specs=in_specs, out_specs=out_specs, check_vma=False)
```

```python
import jax
import jax.numpy as jnp
from jax import lax
from jax.experimental import pallas as pl
from jax.experimental.pallas import tpu as pltpu
from jax.sharding import PartitionSpec as P

OFFMAX = 425
LANE_BITS = 7
LANES = 1 << LANE_BITS
SUBLANES = 8
SMEM = pl.BlockSpec(memory_space=pltpu.SMEM)
VMEM = pl.BlockSpec(memory_space=pltpu.VMEM)
HBM = pl.BlockSpec(memory_space=pltpu.HBM)


def padded_rows(rows):
    return -(-rows // SUBLANES) * SUBLANES


def chunks_of(length, step):
    return (length + 2 * step - 2) // step


def limit(mib):
    return pltpu.CompilerParams(vmem_limit_bytes=mib << 20)


def weights_kernel(
    off_hbm, avail_hbm, templates_ref, weights_ref, inv_ref, coded_ref, off_ref, avail_ref, lines_ref, chunks_ref, sem
):
    templ_here, channels_here, length = templates_ref.shape
    step = LANES // templ_here
    chunks = weights_ref.shape[1] // step
    groups = lines_ref.shape[0]
    width = templ_here * LANES
    bf16, f32 = jnp.bfloat16, jnp.float32
    small = [
        pltpu.make_async_copy(off_hbm, off_ref, sem.at[0]),
        pltpu.make_async_copy(avail_hbm, avail_ref, sem.at[1]),
    ]
    for copy in small:
        copy.start()
    lines_ref[...] = jnp.zeros_like(lines_ref)
    for t in range(templ_here):
        shapes = templates_ref[t]
        centred = shapes - jnp.sum(shapes, axis=1, keepdims=True) / length
        energy = jnp.sum(centred * centred, axis=1, keepdims=True)
        inv_ref[:, t * step : (t + 1) * step] = jnp.broadcast_to(lax.rsqrt(energy + 1e-05), (channels_here, step))
        for q in range(groups):
            here = min(LANES, length - q * LANES)
            lines_ref[q, :channels_here, t * LANES : t * LANES + here] = centred[:, q * LANES : q * LANES + here]
    col = lax.broadcasted_iota(jnp.int32, (1, width), 1)
    source = LANES * ((col % LANES) // step) + step * (col // LANES) + step - 1 - col % step
    pick = (lax.broadcasted_iota(jnp.int32, (width, width), 0) == source).astype(f32).astype(bf16)
    lines = lines_ref[...].reshape(groups * lines_ref.shape[1], width).astype(bf16)
    picked = jnp.dot(lines, pick, preferred_element_type=f32)
    rows = lines_ref.shape[1]
    for m in range(chunks_ref.shape[0]):
        q, i = divmod(m, templ_here)
        chunks_ref[m] = picked[q * rows : (q + 1) * rows, i * LANES : (i + 1) * LANES]

    row = lax.broadcasted_iota(jnp.int32, (step, LANES), 0)
    inside = lax.broadcasted_iota(jnp.int32, (step, LANES), 1) % step <= row

    for c in range(channels_here):
        before = jnp.zeros((step, LANES), f32)
        for m in range(chunks):
            if m * step < length:
                line = jnp.broadcast_to(chunks_ref[m, c : c + 1, :], (step, LANES))
                here = pltpu.roll(line, LANES - step + 1, 1, stride=1, stride_axis=0)
                following = pltpu.roll(line, 1, 1, stride=1, stride_axis=0)
            else:
                here = following = jnp.zeros((step, LANES), f32)
            weights_ref[c, m * step : (m + 1) * step, :] = jnp.where(inside, here, before).astype(bf16)
            before = following
    for copy in small:
        copy.wait()
    coded_ref[...] = 2 * off_ref[...] + avail_ref[...]


def stack_kernel(
    coded_ref, inv_ref, records_ref, weights_ref, out_ref,
    picks_ref, pieces_ref, tails_ref, totals_ref, heads_ref, sem, *slots,
    length,
):
    templ_here, channels_here = coded_ref.shape
    step = LANES // templ_here
    blocks = tails_ref.shape[1] - SUBLANES
    framed = slots[: len(slots) // 2]
    moved = slots[len(slots) // 2 :]
    pitch = records_ref.shape[0] // blocks
    lag_blocks = out_ref.shape[0] // templ_here
    taps = weights_ref.shape[1] // LANES
    bf16, f32 = jnp.bfloat16, jnp.float32
    picks = pltpu.make_async_copy(coded_ref, picks_ref, sem)
    picks.start()
    row = lax.broadcasted_iota(jnp.int32, (LANES, LANES), 0)
    col = lax.broadcasted_iota(jnp.int32, (LANES, LANES), 1)
    turn = LANES - length % LANES
    kinds = (row >= col, row >= 0, row < (col - turn) % LANES)
    adder = jnp.concatenate([kind.astype(f32) for kind in kinds], axis=1).astype(bf16)
    adder = jnp.concatenate([adder, adder], axis=0)

    picks.wait()

    def block_sums():
        for c in range(channels_here):
            x = records_ref[pl.ds(c, blocks, stride=pitch), :]
            for k, v in enumerate((x, x * x)):
                rows = pl.ds((2 * c + k) * blocks, blocks)
                high = v.astype(bf16)
                pieces_ref[rows, 0:LANES] = high
                pieces_ref[rows, LANES : 2 * LANES] = (v - high.astype(f32)).astype(bf16)
        sums = jnp.dot(pieces_ref[...], adder, preferred_element_type=f32)
        count = 2 * channels_here
        for k, ref in enumerate((tails_ref, totals_ref, heads_ref)):
            ref[:, :blocks, :] = sums[:, k * LANES : (k + 1) * LANES].reshape(count, blocks, LANES)
            ref[:, blocks:, :] = jnp.zeros((count, SUBLANES, LANES), f32)

    stacks = [jnp.zeros((lag_blocks, LANES), f32) for _ in range(templ_here)]
    for ref in framed:
        ref[blocks:, :] = jnp.zeros((SUBLANES, LANES), f32)

    whole = length // LANES
    lane = lax.broadcasted_iota(jnp.int32, (blocks, LANES), 1)
    lag_lane = lax.broadcasted_iota(jnp.int32, (lag_blocks, LANES), 1)

    def window_sum(index):
        def at(ref, i):
            return ref[index, i : i + blocks, :]

        total = at(tails_ref, 0)
        for i in range(1, whole):
            total = total + at(totals_ref, i)
        ends = jnp.where(lane < turn, at(heads_ref, whole), at(totals_ref, whole) + at(heads_ref, whole + 1))
        return total + ends

    def regroup(arrays, group):
        count = len(arrays)
        distance = 1
        while distance < count:
            kept = (lane // group) // distance % 2 == 0
            swapped = list(arrays)
            for r in range(count):
                if r // distance % 2 == 0:
                    a, b = arrays[r], arrays[r + distance]
                    shift = group * distance
                    swapped[r] = jnp.where(kept, a, pltpu.roll(b, shift, 1))
                    swapped[r + distance] = jnp.where(kept, pltpu.roll(a, LANES - shift, 1), b)
            arrays = swapped
            distance *= 2
        return arrays

    def regrouped(c):
        slot = c * templ_here
        here = records_ref[pl.ds(c, blocks, stride=pitch), :]
        framed[slot][:blocks, :] = here
        for r in range(1, templ_here):
            ref = framed[slot + r]
            turned = pltpu.roll(here, LANES - r * step, 1)
            ref[:blocks, :] = turned
            ref[:blocks, :] = jnp.where(lane < LANES - r * step, turned, ref[1 : blocks + 1, :])
        frames = jnp.concatenate(
            [
                jnp.concatenate([framed[slot + r][q : q + blocks, :].astype(bf16) for q in range(taps)], axis=1)
                for r in range(templ_here)
            ],
            axis=0,
        )
        product = jnp.dot(frames, weights_ref[c], preferred_element_type=f32) * inv_ref[c : c + 1, :]
        return regroup([product[r * blocks : (r + 1) * blocks, :] for r in range(templ_here)], step)

    def picked(c, correlated, stacks):
        slot = c * templ_here
        first = window_sum(2 * c)
        second = window_sum(2 * c + 1)
        scale = lax.rsqrt(second - first * first / length + 1e-05)
        for t in range(templ_here):
            pick = picks_ref[t, c]
            down = pick >> LANE_BITS + 1
            over = (pick >> 1) & (LANES - 1)
            ref = moved[slot + t]
            ref[:blocks, :] = pltpu.roll(correlated[t] * scale, (LANES - over) & (LANES - 1), 1)
            near = ref[pl.ds(down, lag_blocks), :]
            far = ref[pl.ds(down + 1, lag_blocks), :]
            lags = jnp.where(lag_lane < LANES - over, near, far)
            stacks[t] = stacks[t] + lags * (pick & 1).astype(f32)

    block_sums()
    for c in range(channels_here):
        picked(c, regrouped(c), stacks)

    for t in range(templ_here):
        out_ref[t * lag_blocks : (t + 1) * lag_blocks, :] = stacks[t]


def finish_kernel(place_ref, *refs):
    *parts, out_ref, stack_ref = refs
    templ_here, share = out_ref.shape
    lag_blocks = stack_ref.shape[0] // templ_here
    own = share // LANES
    for t in range(templ_here):
        rows = pl.ds(t * lag_blocks, lag_blocks)
        stack = parts[0][rows, :].astype(jnp.float32)
        for part in parts[1:]:
            stack = stack + part[rows, :].astype(jnp.float32)
        stack_ref[rows, :] = stack
        power = jnp.sum(jnp.sum(stack * stack, axis=0, keepdims=True), axis=1, keepdims=True)
        unit = 1.0 / jnp.sqrt(power / (lag_blocks * LANES) + 1e-05)
        for i in range(own):
            line = stack_ref[pl.ds(t * lag_blocks + place_ref[0] * own + i, 1), :]
            out_ref[t : t + 1, i * LANES : (i + 1) * LANES] = line * unit


def spread_records(records, count):
    channels_here, block_len = records.shape
    return jnp.broadcast_to(records.reshape(1, channels_here, 1, block_len), (count, channels_here, 1, block_len))


def prepared_weights(templates, offsets, available):
    templ_here, channels_here, length = templates.shape
    step = LANES // templ_here
    groups = -(-length // LANES)
    rows = padded_rows(channels_here)
    lines = pltpu.VMEM((groups, rows, templ_here * LANES), jnp.float32)
    chunks = pltpu.VMEM((groups * templ_here, rows, LANES), jnp.float32)
    return pl.pallas_call(
        weights_kernel,
        out_shape=(
            jax.ShapeDtypeStruct((channels_here, chunks_of(length, step) * step, LANES), jnp.bfloat16),
            jax.ShapeDtypeStruct((channels_here, LANES), jnp.float32),
            jax.ShapeDtypeStruct(offsets.shape, jnp.int32),
        ),
        in_specs=[HBM, HBM, VMEM],
        out_specs=(VMEM, VMEM, VMEM),
        scratch_shapes=[
            pltpu.VMEM(offsets.shape, jnp.int32),
            pltpu.VMEM(offsets.shape, jnp.int32),
            lines,
            chunks,
            pltpu.SemaphoreType.DMA((2,)),
        ],
        compiler_params=limit(16),
        name="prepare_weights",
    )(*(pltpu.with_memory_space_constraint(a, pltpu.HBM) for a in (offsets, available)), templates)


def partial_stacks(blocks, count, weights, inv, coded, lag_count, length):
    templ_here, channels_here = coded.shape
    lag_blocks = lag_count // LANES
    total_rows = 2 * channels_here * count
    f32 = jnp.float32
    return pl.pallas_call(
        lambda *refs: stack_kernel(*refs, length=length),
        out_shape=jax.ShapeDtypeStruct((templ_here * lag_blocks, LANES), f32),
        in_specs=[VMEM, VMEM, VMEM, VMEM],
        out_specs=VMEM,
        scratch_shapes=[
            pltpu.SMEM(coded.shape, coded.dtype),
            pltpu.VMEM((total_rows, 2 * LANES), jnp.bfloat16),
            pltpu.VMEM((2 * channels_here, count + SUBLANES, LANES), f32),
            pltpu.VMEM((2 * channels_here, count + SUBLANES, LANES), f32),
            pltpu.VMEM((2 * channels_here, count + SUBLANES, LANES), f32),
            pltpu.SemaphoreType.DMA(()),
        ]
        + [pltpu.VMEM((count + SUBLANES, LANES), f32)] * (2 * channels_here * templ_here),
        compiler_params=limit(24),
        name="stack_channels",
    )(coded, inv, blocks, weights)


def finished(place, parts, templ_here, share):
    return pl.pallas_call(
        finish_kernel,
        out_shape=jax.ShapeDtypeStruct((templ_here, share), jnp.float32),
        in_specs=[SMEM] + [VMEM] * len(parts),
        out_specs=VMEM,
        scratch_shapes=[pltpu.VMEM(parts[0].shape, jnp.float32)],
        compiler_params=limit(4),
        name="finish",
    )(place, *parts)


ORDER = (1, 2, 6)


def swapped(array, distance):
    return lax.ppermute(array, "sta", [(i, i ^ distance) for i in range(lax.axis_size("sta"))])


def shards(records, templates, offsets, available):
    block_len = records.shape[1]
    templ_here, _, length = templates.shape
    count = lax.axis_size("tmpl")
    shares = lax.axis_size("sta")
    lag_count = block_len * count - OFFMAX - length + 1
    blocks = lax.all_to_all(spread_records(records, count), "tmpl", 0, 0, tiled=True)
    weights, inv, coded = prepared_weights(templates, offsets, available)
    mine = partial_stacks(blocks.reshape(-1, block_len), count, weights, inv, coded, lag_count, length)
    place = lax.axis_index("sta").reshape(1).astype(jnp.int32)
    bf16, f32 = jnp.bfloat16, jnp.float32
    parts = [mine]
    for distance in ORDER:
        mine = parts[0] if len(parts) == 1 else parts[0] + parts[1].astype(f32)
        parts = [mine, swapped(mine if distance == 1 else mine.astype(bf16), distance)]
    return finished(place, parts, templ_here, lag_count // shares)


def solution(mesh):
    in_specs = (P("sta", "tmpl"), P("tmpl", "sta", None), P("tmpl", "sta"), P("tmpl", "sta"))
    out_specs = P("tmpl", "sta")
    return jax.shard_map(shards, mesh=mesh, in_specs=in_specs, out_specs=out_specs, check_vma=False)
```

```python
import jax
import jax.numpy as jnp
from jax import lax
from jax.experimental import pallas as pl
from jax.experimental.pallas import tpu as pltpu
from jax.sharding import PartitionSpec as P

OFFMAX = 425
LANE_BITS = 7
LANES = 1 << LANE_BITS
SUBLANES = 8
SMEM = pl.BlockSpec(memory_space=pltpu.SMEM)
VMEM = pl.BlockSpec(memory_space=pltpu.VMEM)
HBM = pl.BlockSpec(memory_space=pltpu.HBM)


def padded_rows(rows):
    return -(-rows // SUBLANES) * SUBLANES


def chunks_of(length, step):
    return (length + 2 * step - 2) // step


def limit(mib):
    return pltpu.CompilerParams(vmem_limit_bytes=mib << 20)


def weights_kernel(
    off_hbm, avail_hbm, templates_ref, weights_ref, inv_ref, coded_ref, off_ref, avail_ref, lines_ref, chunks_ref, sem
):
    templ_here, channels_here, length = templates_ref.shape
    step = LANES // templ_here
    chunks = weights_ref.shape[1] // step
    groups = lines_ref.shape[0]
    width = templ_here * LANES
    bf16, f32 = jnp.bfloat16, jnp.float32
    small = [
        pltpu.make_async_copy(off_hbm, off_ref, sem.at[0]),
        pltpu.make_async_copy(avail_hbm, avail_ref, sem.at[1]),
    ]
    for copy in small:
        copy.start()
    lines_ref[...] = jnp.zeros_like(lines_ref)
    for t in range(templ_here):
        shapes = templates_ref[t]
        centred = shapes - jnp.sum(shapes, axis=1, keepdims=True) / length
        energy = jnp.sum(centred * centred, axis=1, keepdims=True)
        inv_ref[:, t * step : (t + 1) * step] = jnp.broadcast_to(lax.rsqrt(energy + 1e-05), (channels_here, step))
        for q in range(groups):
            here = min(LANES, length - q * LANES)
            lines_ref[q, :channels_here, t * LANES : t * LANES + here] = centred[:, q * LANES : q * LANES + here]
    col = lax.broadcasted_iota(jnp.int32, (1, width), 1)
    source = LANES * ((col % LANES) // step) + step * (col // LANES) + step - 1 - col % step
    pick = (lax.broadcasted_iota(jnp.int32, (width, width), 0) == source).astype(f32).astype(bf16)
    lines = lines_ref[...].reshape(groups * lines_ref.shape[1], width).astype(bf16)
    picked = jnp.dot(lines, pick, preferred_element_type=f32)
    rows = lines_ref.shape[1]
    for m in range(chunks_ref.shape[0]):
        q, i = divmod(m, templ_here)
        chunks_ref[m] = picked[q * rows : (q + 1) * rows, i * LANES : (i + 1) * LANES]

    row = lax.broadcasted_iota(jnp.int32, (step, LANES), 0)
    inside = lax.broadcasted_iota(jnp.int32, (step, LANES), 1) % step <= row

    for c in range(channels_here):
        before = jnp.zeros((step, LANES), f32)
        for m in range(chunks):
            if m * step < length:
                line = jnp.broadcast_to(chunks_ref[m, c : c + 1, :], (step, LANES))
                here = pltpu.roll(line, LANES - step + 1, 1, stride=1, stride_axis=0)
                following = pltpu.roll(line, 1, 1, stride=1, stride_axis=0)
            else:
                here = following = jnp.zeros((step, LANES), f32)
            weights_ref[c, m * step : (m + 1) * step, :] = jnp.where(inside, here, before).astype(bf16)
            before = following
    for copy in small:
        copy.wait()
    coded_ref[...] = 2 * off_ref[...] + avail_ref[...]


def stack_kernel(
    coded_ref, inv_ref, records_ref, weights_ref, out_ref,
    picks_ref, pieces_ref, tails_ref, totals_ref, heads_ref, sem, *slots,
    length,
):
    templ_here, channels_here = coded_ref.shape
    step = LANES // templ_here
    blocks = tails_ref.shape[1] - SUBLANES
    framed = slots[: len(slots) // 2]
    moved = slots[len(slots) // 2 :]
    pitch = records_ref.shape[0] // blocks
    lag_blocks = out_ref.shape[0] // templ_here
    taps = weights_ref.shape[1] // LANES
    bf16, f32 = jnp.bfloat16, jnp.float32
    picks = pltpu.make_async_copy(coded_ref, picks_ref, sem)
    picks.start()
    row = lax.broadcasted_iota(jnp.int32, (LANES, LANES), 0)
    col = lax.broadcasted_iota(jnp.int32, (LANES, LANES), 1)
    turn = LANES - length % LANES
    kinds = (row >= col, row >= 0, row < (col - turn) % LANES)
    adder = jnp.concatenate([kind.astype(f32) for kind in kinds], axis=1).astype(bf16)
    adder = jnp.concatenate([adder, adder], axis=0)

    picks.wait()

    def block_sums():
        for c in range(channels_here):
            x = records_ref[pl.ds(c, blocks, stride=pitch), :]
            for k, v in enumerate((x, x * x)):
                rows = pl.ds((2 * c + k) * blocks, blocks)
                high = v.astype(bf16)
                pieces_ref[rows, 0:LANES] = high
                pieces_ref[rows, LANES : 2 * LANES] = (v - high.astype(f32)).astype(bf16)
        sums = jnp.dot(pieces_ref[...], adder, preferred_element_type=f32)
        count = 2 * channels_here
        for k, ref in enumerate((tails_ref, totals_ref, heads_ref)):
            ref[:, :blocks, :] = sums[:, k * LANES : (k + 1) * LANES].reshape(count, blocks, LANES)
            ref[:, blocks:, :] = jnp.zeros((count, SUBLANES, LANES), f32)

    stacks = [jnp.zeros((lag_blocks, LANES), f32) for _ in range(templ_here)]
    for ref in framed:
        ref[blocks:, :] = jnp.zeros((SUBLANES, LANES), f32)

    whole = length // LANES
    lane = lax.broadcasted_iota(jnp.int32, (blocks, LANES), 1)
    lag_lane = lax.broadcasted_iota(jnp.int32, (lag_blocks, LANES), 1)

    def window_sum(index):
        def at(ref, i):
            return ref[index, i : i + blocks, :]

        total = at(tails_ref, 0)
        for i in range(1, whole):
            total = total + at(totals_ref, i)
        ends = jnp.where(lane < turn, at(heads_ref, whole), at(totals_ref, whole) + at(heads_ref, whole + 1))
        return total + ends

    def diagonals(arrays):
        count = len(arrays)
        moved_on = [arrays[0]] + [pltpu.roll(arrays[r], r * step, 1) for r in range(1, count)]
        block = lane // step
        out = []
        for t in range(count):
            line = moved_on[0]
            for r in range(1, count):
                line = jnp.where(block == (t + r) % count, moved_on[r], line)
            out.append(line)
        return out

    def regrouped(c):
        slot = c * templ_here
        here = records_ref[pl.ds(c, blocks, stride=pitch), :]
        framed[slot][:blocks, :] = here
        for r in range(1, templ_here):
            ref = framed[slot + r]
            turned = pltpu.roll(here, LANES - r * step, 1)
            ref[:blocks, :] = turned
            ref[:blocks, :] = jnp.where(lane < LANES - r * step, turned, ref[1 : blocks + 1, :])
        frames = jnp.concatenate(
            [
                jnp.concatenate([framed[slot + r][q : q + blocks, :].astype(bf16) for q in range(taps)], axis=1)
                for r in range(templ_here)
            ],
            axis=0,
        )
        product = jnp.dot(frames, weights_ref[c], preferred_element_type=f32) * inv_ref[c : c + 1, :]
        return diagonals([product[r * blocks : (r + 1) * blocks, :] for r in range(templ_here)])

    def picked(c, correlated, stacks):
        slot = c * templ_here
        first = window_sum(2 * c)
        second = window_sum(2 * c + 1)
        scale = lax.rsqrt(second - first * first / length + 1e-05)
        for t in range(templ_here):
            pick = picks_ref[t, c]
            down = pick >> LANE_BITS + 1
            over = (pick >> 1) & (LANES - 1)
            ref = moved[slot + t]
            turned = pltpu.roll(scale, t * step, 1) if t else scale
            ref[:blocks, :] = pltpu.roll(correlated[t] * turned, (2 * LANES - t * step - over) & (LANES - 1), 1)
            near = ref[pl.ds(down, lag_blocks), :]
            far = ref[pl.ds(down + 1, lag_blocks), :]
            lags = jnp.where(lag_lane < LANES - over, near, far)
            stacks[t] = stacks[t] + lags * (pick & 1).astype(f32)

    block_sums()
    for c in range(channels_here):
        picked(c, regrouped(c), stacks)

    for t in range(templ_here):
        out_ref[t * lag_blocks : (t + 1) * lag_blocks, :] = stacks[t]


def finish_kernel(place_ref, *refs):
    *parts, out_ref, stack_ref = refs
    templ_here, share = out_ref.shape
    lag_blocks = stack_ref.shape[0] // templ_here
    own = share // LANES
    for t in range(templ_here):
        rows = pl.ds(t * lag_blocks, lag_blocks)
        stack = parts[0][rows, :].astype(jnp.float32)
        for part in parts[1:]:
            stack = stack + part[rows, :].astype(jnp.float32)
        stack_ref[rows, :] = stack
        power = jnp.sum(jnp.sum(stack * stack, axis=0, keepdims=True), axis=1, keepdims=True)
        unit = 1.0 / jnp.sqrt(power / (lag_blocks * LANES) + 1e-05)
        for i in range(own):
            line = stack_ref[pl.ds(t * lag_blocks + place_ref[0] * own + i, 1), :]
            out_ref[t : t + 1, i * LANES : (i + 1) * LANES] = line * unit


def spread_records(records, count):
    channels_here, block_len = records.shape
    return jnp.broadcast_to(records.reshape(1, channels_here, 1, block_len), (count, channels_here, 1, block_len))


def prepared_weights(templates, offsets, available):
    templ_here, channels_here, length = templates.shape
    step = LANES // templ_here
    groups = -(-length // LANES)
    rows = padded_rows(channels_here)
    lines = pltpu.VMEM((groups, rows, templ_here * LANES), jnp.float32)
    chunks = pltpu.VMEM((groups * templ_here, rows, LANES), jnp.float32)
    return pl.pallas_call(
        weights_kernel,
        out_shape=(
            jax.ShapeDtypeStruct((channels_here, chunks_of(length, step) * step, LANES), jnp.bfloat16),
            jax.ShapeDtypeStruct((channels_here, LANES), jnp.float32),
            jax.ShapeDtypeStruct(offsets.shape, jnp.int32),
        ),
        in_specs=[HBM, HBM, VMEM],
        out_specs=(VMEM, VMEM, VMEM),
        scratch_shapes=[
            pltpu.VMEM(offsets.shape, jnp.int32),
            pltpu.VMEM(offsets.shape, jnp.int32),
            lines,
            chunks,
            pltpu.SemaphoreType.DMA((2,)),
        ],
        compiler_params=limit(16),
        name="prepare_weights",
    )(*(pltpu.with_memory_space_constraint(a, pltpu.HBM) for a in (offsets, available)), templates)


def partial_stacks(blocks, count, weights, inv, coded, lag_count, length):
    templ_here, channels_here = coded.shape
    lag_blocks = lag_count // LANES
    total_rows = 2 * channels_here * count
    f32 = jnp.float32
    return pl.pallas_call(
        lambda *refs: stack_kernel(*refs, length=length),
        out_shape=jax.ShapeDtypeStruct((templ_here * lag_blocks, LANES), f32),
        in_specs=[VMEM, VMEM, VMEM, VMEM],
        out_specs=VMEM,
        scratch_shapes=[
            pltpu.SMEM(coded.shape, coded.dtype),
            pltpu.VMEM((total_rows, 2 * LANES), jnp.bfloat16),
            pltpu.VMEM((2 * channels_here, count + SUBLANES, LANES), f32),
            pltpu.VMEM((2 * channels_here, count + SUBLANES, LANES), f32),
            pltpu.VMEM((2 * channels_here, count + SUBLANES, LANES), f32),
            pltpu.SemaphoreType.DMA(()),
        ]
        + [pltpu.VMEM((count + SUBLANES, LANES), f32)] * (2 * channels_here * templ_here),
        compiler_params=limit(24),
        name="stack_channels",
    )(coded, inv, blocks, weights)


def finished(place, parts, templ_here, share):
    return pl.pallas_call(
        finish_kernel,
        out_shape=jax.ShapeDtypeStruct((templ_here, share), jnp.float32),
        in_specs=[SMEM] + [VMEM] * len(parts),
        out_specs=VMEM,
        scratch_shapes=[pltpu.VMEM(parts[0].shape, jnp.float32)],
        compiler_params=limit(4),
        name="finish",
    )(place, *parts)


ORDER = (1, 2, 6)


def swapped(array, distance):
    return lax.ppermute(array, "sta", [(i, i ^ distance) for i in range(lax.axis_size("sta"))])


def shards(records, templates, offsets, available):
    block_len = records.shape[1]
    templ_here, _, length = templates.shape
    count = lax.axis_size("tmpl")
    shares = lax.axis_size("sta")
    lag_count = block_len * count - OFFMAX - length + 1
    blocks = lax.all_to_all(spread_records(records, count), "tmpl", 0, 0, tiled=True)
    weights, inv, coded = prepared_weights(templates, offsets, available)
    mine = partial_stacks(blocks.reshape(-1, block_len), count, weights, inv, coded, lag_count, length)
    place = lax.axis_index("sta").reshape(1).astype(jnp.int32)
    bf16, f32 = jnp.bfloat16, jnp.float32
    parts = [mine]
    for distance in ORDER:
        mine = parts[0] if len(parts) == 1 else parts[0] + parts[1].astype(f32)
        parts = [mine, swapped(mine if distance == 1 else mine.astype(bf16), distance)]
    return finished(place, parts, templ_here, lag_count // shares)


def solution(mesh):
    in_specs = (P("sta", "tmpl"), P("tmpl", "sta", None), P("tmpl", "sta"), P("tmpl", "sta"))
    out_specs = P("tmpl", "sta")
    return jax.shard_map(shards, mesh=mesh, in_specs=in_specs, out_specs=out_specs, check_vma=False)
```

```python
import jax
import jax.numpy as jnp
from jax import lax
from jax.experimental import pallas as pl
from jax.experimental.pallas import tpu as pltpu
from jax.sharding import PartitionSpec as P

OFFMAX = 425
LANE_BITS = 7
LANES = 1 << LANE_BITS
SUBLANES = 8
SMEM = pl.BlockSpec(memory_space=pltpu.SMEM)
VMEM = pl.BlockSpec(memory_space=pltpu.VMEM)
HBM = pl.BlockSpec(memory_space=pltpu.HBM)


def padded_rows(rows):
    return -(-rows // SUBLANES) * SUBLANES


def chunks_of(length, step):
    return (length + 2 * step - 2) // step


def limit(mib):
    return pltpu.CompilerParams(vmem_limit_bytes=mib << 20)


def weights_kernel(
    off_hbm, avail_hbm, templates_ref, weights_ref, inv_ref, coded_ref, off_ref, avail_ref, lines_ref, chunks_ref, sem
):
    templ_here, channels_here, length = templates_ref.shape
    step = LANES // templ_here
    chunks = weights_ref.shape[1] // step
    groups = lines_ref.shape[0]
    width = templ_here * LANES
    bf16, f32 = jnp.bfloat16, jnp.float32
    small = [
        pltpu.make_async_copy(off_hbm, off_ref, sem.at[0]),
        pltpu.make_async_copy(avail_hbm, avail_ref, sem.at[1]),
    ]
    for copy in small:
        copy.start()
    lines_ref[...] = jnp.zeros_like(lines_ref)
    for t in range(templ_here):
        shapes = templates_ref[t]
        centred = shapes - jnp.sum(shapes, axis=1, keepdims=True) / length
        energy = jnp.sum(centred * centred, axis=1, keepdims=True)
        inv_ref[:, t * step : (t + 1) * step] = jnp.broadcast_to(lax.rsqrt(energy + 1e-05), (channels_here, step))
        for q in range(groups):
            here = min(LANES, length - q * LANES)
            lines_ref[q, :channels_here, t * LANES : t * LANES + here] = centred[:, q * LANES : q * LANES + here]
    col = lax.broadcasted_iota(jnp.int32, (1, width), 1)
    source = LANES * ((col % LANES) // step) + step * (col // LANES) + step - 1 - col % step
    pick = (lax.broadcasted_iota(jnp.int32, (width, width), 0) == source).astype(f32).astype(bf16)
    lines = lines_ref[...].reshape(groups * lines_ref.shape[1], width).astype(bf16)
    picked = jnp.dot(lines, pick, preferred_element_type=f32)
    rows = lines_ref.shape[1]
    for m in range(chunks_ref.shape[0]):
        q, i = divmod(m, templ_here)
        chunks_ref[m] = picked[q * rows : (q + 1) * rows, i * LANES : (i + 1) * LANES]

    row = lax.broadcasted_iota(jnp.int32, (step, LANES), 0)
    inside = lax.broadcasted_iota(jnp.int32, (step, LANES), 1) % step <= row

    for c in range(channels_here):
        before = jnp.zeros((step, LANES), f32)
        for m in range(chunks):
            if m * step < length:
                line = jnp.broadcast_to(chunks_ref[m, c : c + 1, :], (step, LANES))
                here = pltpu.roll(line, LANES - step + 1, 1, stride=1, stride_axis=0)
                following = pltpu.roll(line, 1, 1, stride=1, stride_axis=0)
            else:
                here = following = jnp.zeros((step, LANES), f32)
            weights_ref[c, m * step : (m + 1) * step, :] = jnp.where(inside, here, before).astype(bf16)
            before = following
    for copy in small:
        copy.wait()
    coded_ref[...] = 2 * off_ref[...] + avail_ref[...]


def stack_kernel(
    coded_ref, inv_ref, records_ref, weights_ref, out_ref,
    picks_ref, pieces_ref, tails_ref, totals_ref, heads_ref, sem, *slots,
    length,
):
    templ_here, channels_here = coded_ref.shape
    step = LANES // templ_here
    blocks = tails_ref.shape[1] - SUBLANES
    framed = slots[: len(slots) // 2]
    moved = slots[len(slots) // 2 :]
    pitch = records_ref.shape[0] // blocks
    lag_blocks = out_ref.shape[0] // templ_here
    taps = weights_ref.shape[1] // LANES
    bf16, f32 = jnp.bfloat16, jnp.float32
    picks = pltpu.make_async_copy(coded_ref, picks_ref, sem)
    picks.start()
    row = lax.broadcasted_iota(jnp.int32, (LANES, LANES), 0)
    col = lax.broadcasted_iota(jnp.int32, (LANES, LANES), 1)
    turn = LANES - length % LANES
    kinds = (row >= col, row >= 0, row < (col - turn) % LANES)
    adder = jnp.concatenate([kind.astype(f32) for kind in kinds], axis=1).astype(bf16)
    adder = jnp.concatenate([adder, adder], axis=0)

    picks.wait()

    def block_sums():
        for c in range(channels_here):
            x = records_ref[pl.ds(c, blocks, stride=pitch), :]
            for k, v in enumerate((x, x * x)):
                rows = pl.ds((2 * c + k) * blocks, blocks)
                high = v.astype(bf16)
                pieces_ref[rows, 0:LANES] = high
                pieces_ref[rows, LANES : 2 * LANES] = (v - high.astype(f32)).astype(bf16)
        sums = jnp.dot(pieces_ref[...], adder, preferred_element_type=f32)
        count = 2 * channels_here
        for k, ref in enumerate((tails_ref, totals_ref, heads_ref)):
            ref[:, :blocks, :] = sums[:, k * LANES : (k + 1) * LANES].reshape(count, blocks, LANES)
            ref[:, blocks:, :] = jnp.zeros((count, SUBLANES, LANES), f32)

    stacks = [jnp.zeros((lag_blocks, LANES), f32) for _ in range(templ_here)]
    for ref in framed:
        ref[blocks:, :] = jnp.zeros((SUBLANES, LANES), f32)

    whole = length // LANES
    lane = lax.broadcasted_iota(jnp.int32, (blocks, LANES), 1)
    lag_lane = lax.broadcasted_iota(jnp.int32, (lag_blocks, LANES), 1)

    def window_sum(index):
        def at(ref, i):
            return ref[index, i : i + blocks, :]

        total = at(tails_ref, 0)
        for i in range(1, whole):
            total = total + at(totals_ref, i)
        ends = jnp.where(lane < turn, at(heads_ref, whole), at(totals_ref, whole) + at(heads_ref, whole + 1))
        return total + ends

    def diagonals(arrays):
        count = len(arrays)
        moved_on = [arrays[0]] + [pltpu.roll(arrays[r], r * step, 1) for r in range(1, count)]
        block = lane // step
        out = []
        for t in range(count):
            line = moved_on[0]
            for r in range(1, count):
                line = jnp.where(block == (t + r) % count, moved_on[r], line)
            out.append(line)
        return out

    def regrouped(c):
        slot = c * templ_here
        here = records_ref[pl.ds(c, blocks, stride=pitch), :]
        framed[slot][:blocks, :] = here
        for r in range(1, templ_here):
            ref = framed[slot + r]
            turned = pltpu.roll(here, LANES - r * step, 1)
            ref[:blocks, :] = turned
            ref[:blocks, :] = jnp.where(lane < LANES - r * step, turned, ref[1 : blocks + 1, :])
        frames = jnp.concatenate(
            [
                jnp.concatenate([framed[slot + r][q : q + blocks, :].astype(bf16) for q in range(taps)], axis=1)
                for r in range(templ_here)
            ],
            axis=0,
        )
        product = jnp.dot(frames, weights_ref[c], preferred_element_type=f32) * inv_ref[c : c + 1, :]
        return diagonals([product[r * blocks : (r + 1) * blocks, :] for r in range(templ_here)])

    def picked(c, correlated, stacks):
        slot = c * templ_here
        first = window_sum(2 * c)
        second = window_sum(2 * c + 1)
        scale = lax.rsqrt(second - first * first / length + 1e-05)
        for t in range(templ_here):
            pick = picks_ref[t, c]
            down = pick >> LANE_BITS + 1
            over = (pick >> 1) & (LANES - 1)
            ref = moved[slot + t]
            turned = pltpu.roll(scale, t * step, 1) if t else scale
            ref[:blocks, :] = pltpu.roll(correlated[t] * turned, (2 * LANES - t * step - over) & (LANES - 1), 1)
            near = ref[pl.ds(down, lag_blocks), :]
            far = ref[pl.ds(down + 1, lag_blocks), :]
            lags = jnp.where(lag_lane < LANES - over, near, far)
            stacks[t] = stacks[t] + lags * (pick & 1).astype(f32)

    block_sums()
    for c in range(channels_here):
        picked(c, regrouped(c), stacks)

    for t in range(templ_here):
        out_ref[t * lag_blocks : (t + 1) * lag_blocks, :] = stacks[t]


def finish_kernel(place_ref, *refs):
    *parts, out_ref, stack_ref = refs
    templ_here, share = out_ref.shape
    lag_blocks = stack_ref.shape[0] // templ_here
    own = share // LANES
    for t in range(templ_here):
        rows = pl.ds(t * lag_blocks, lag_blocks)
        stack = parts[0][rows, :].astype(jnp.float32)
        for part in parts[1:]:
            stack = stack + part[rows, :].astype(jnp.float32)
        stack_ref[rows, :] = stack
        power = jnp.sum(jnp.sum(stack * stack, axis=0, keepdims=True), axis=1, keepdims=True)
        unit = 1.0 / jnp.sqrt(power / (lag_blocks * LANES) + 1e-05)
        for i in range(own):
            line = stack_ref[pl.ds(t * lag_blocks + place_ref[0] * own + i, 1), :]
            out_ref[t : t + 1, i * LANES : (i + 1) * LANES] = line * unit


def spread_kernel(records_ref, out_ref):
    channels_here = records_ref.shape[0]
    block = records_ref[...]
    for i in range(out_ref.shape[0] // channels_here):
        out_ref[i * channels_here : (i + 1) * channels_here, :] = block


def spread_records(records, count):
    channels_here, block_len = records.shape
    copies = pl.pallas_call(
        spread_kernel,
        out_shape=jax.ShapeDtypeStruct((count * channels_here, block_len), records.dtype),
        in_specs=[VMEM],
        out_specs=VMEM,
        compiler_params=limit(2),
        name="spread_records",
    )(records)
    return copies.reshape(count, channels_here, 1, block_len)


def prepared_weights(templates, offsets, available):
    templ_here, channels_here, length = templates.shape
    step = LANES // templ_here
    groups = -(-length // LANES)
    rows = padded_rows(channels_here)
    lines = pltpu.VMEM((groups, rows, templ_here * LANES), jnp.float32)
    chunks = pltpu.VMEM((groups * templ_here, rows, LANES), jnp.float32)
    return pl.pallas_call(
        weights_kernel,
        out_shape=(
            jax.ShapeDtypeStruct((channels_here, chunks_of(length, step) * step, LANES), jnp.bfloat16),
            jax.ShapeDtypeStruct((channels_here, LANES), jnp.float32),
            jax.ShapeDtypeStruct(offsets.shape, jnp.int32),
        ),
        in_specs=[HBM, HBM, VMEM],
        out_specs=(VMEM, VMEM, VMEM),
        scratch_shapes=[
            pltpu.VMEM(offsets.shape, jnp.int32),
            pltpu.VMEM(offsets.shape, jnp.int32),
            lines,
            chunks,
            pltpu.SemaphoreType.DMA((2,)),
        ],
        compiler_params=limit(16),
        name="prepare_weights",
    )(*(pltpu.with_memory_space_constraint(a, pltpu.HBM) for a in (offsets, available)), templates)


def partial_stacks(blocks, count, weights, inv, coded, lag_count, length):
    templ_here, channels_here = coded.shape
    lag_blocks = lag_count // LANES
    total_rows = 2 * channels_here * count
    f32 = jnp.float32
    return pl.pallas_call(
        lambda *refs: stack_kernel(*refs, length=length),
        out_shape=jax.ShapeDtypeStruct((templ_here * lag_blocks, LANES), f32),
        in_specs=[VMEM, VMEM, VMEM, VMEM],
        out_specs=VMEM,
        scratch_shapes=[
            pltpu.SMEM(coded.shape, coded.dtype),
            pltpu.VMEM((total_rows, 2 * LANES), jnp.bfloat16),
            pltpu.VMEM((2 * channels_here, count + SUBLANES, LANES), f32),
            pltpu.VMEM((2 * channels_here, count + SUBLANES, LANES), f32),
            pltpu.VMEM((2 * channels_here, count + SUBLANES, LANES), f32),
            pltpu.SemaphoreType.DMA(()),
        ]
        + [pltpu.VMEM((count + SUBLANES, LANES), f32)] * (2 * channels_here * templ_here),
        compiler_params=limit(24),
        name="stack_channels",
    )(coded, inv, blocks, weights)


def finished(place, parts, templ_here, share):
    return pl.pallas_call(
        finish_kernel,
        out_shape=jax.ShapeDtypeStruct((templ_here, share), jnp.float32),
        in_specs=[SMEM] + [VMEM] * len(parts),
        out_specs=VMEM,
        scratch_shapes=[pltpu.VMEM(parts[0].shape, jnp.float32)],
        compiler_params=limit(4),
        name="finish",
    )(place, *parts)


ORDER = (1, 2, 6)


def swapped(array, distance):
    return lax.ppermute(array, "sta", [(i, i ^ distance) for i in range(lax.axis_size("sta"))])


def shards(records, templates, offsets, available):
    block_len = records.shape[1]
    templ_here, _, length = templates.shape
    count = lax.axis_size("tmpl")
    shares = lax.axis_size("sta")
    lag_count = block_len * count - OFFMAX - length + 1
    blocks = lax.all_to_all(spread_records(records, count), "tmpl", 0, 0, tiled=True)
    weights, inv, coded = prepared_weights(templates, offsets, available)
    mine = partial_stacks(blocks.reshape(-1, block_len), count, weights, inv, coded, lag_count, length)
    place = lax.axis_index("sta").reshape(1).astype(jnp.int32)
    bf16, f32 = jnp.bfloat16, jnp.float32
    parts = [mine]
    for distance in ORDER:
        mine = parts[0] if len(parts) == 1 else parts[0] + parts[1].astype(f32)
        parts = [mine, swapped(mine if distance == 1 else mine.astype(bf16), distance)]
    return finished(place, parts, templ_here, lag_count // shares)


def solution(mesh):
    in_specs = (P("sta", "tmpl"), P("tmpl", "sta", None), P("tmpl", "sta"), P("tmpl", "sta"))
    out_specs = P("tmpl", "sta")
    return jax.shard_map(shards, mesh=mesh, in_specs=in_specs, out_specs=out_specs, check_vma=False)
```

```python
import jax
import jax.numpy as jnp
from jax import lax
from jax.experimental import pallas as pl
from jax.experimental.pallas import tpu as pltpu
from jax.sharding import PartitionSpec as P

OFFMAX = 425
LANE_BITS = 7
LANES = 1 << LANE_BITS
SUBLANES = 8
SMEM = pl.BlockSpec(memory_space=pltpu.SMEM)
VMEM = pl.BlockSpec(memory_space=pltpu.VMEM)
HBM = pl.BlockSpec(memory_space=pltpu.HBM)


def padded_rows(rows):
    return -(-rows // SUBLANES) * SUBLANES


def chunks_of(length, step):
    return (length + 2 * step - 2) // step


def limit(mib):
    return pltpu.CompilerParams(vmem_limit_bytes=mib << 20)


def weights_kernel(
    off_hbm, avail_hbm, templates_ref, weights_ref, inv_ref, coded_ref, off_ref, avail_ref, lines_ref, chunks_ref, sem
):
    templ_here, channels_here, length = templates_ref.shape
    step = LANES // templ_here
    chunks = weights_ref.shape[1] // step
    groups = lines_ref.shape[0]
    width = templ_here * LANES
    bf16, f32 = jnp.bfloat16, jnp.float32
    small = [
        pltpu.make_async_copy(off_hbm, off_ref, sem.at[0]),
        pltpu.make_async_copy(avail_hbm, avail_ref, sem.at[1]),
    ]
    for copy in small:
        copy.start()
    lines_ref[...] = jnp.zeros_like(lines_ref)
    for t in range(templ_here):
        shapes = templates_ref[t]
        centred = shapes - jnp.sum(shapes, axis=1, keepdims=True) / length
        energy = jnp.sum(centred * centred, axis=1, keepdims=True)
        inv_ref[:, t * step : (t + 1) * step] = jnp.broadcast_to(lax.rsqrt(energy + 1e-05), (channels_here, step))
        for q in range(groups):
            here = min(LANES, length - q * LANES)
            lines_ref[q, :channels_here, t * LANES : t * LANES + here] = centred[:, q * LANES : q * LANES + here]
    col = lax.broadcasted_iota(jnp.int32, (1, width), 1)
    source = LANES * ((col % LANES) // step) + step * (col // LANES) + step - 1 - col % step
    pick = (lax.broadcasted_iota(jnp.int32, (width, width), 0) == source).astype(f32).astype(bf16)
    lines = lines_ref[...].reshape(groups * lines_ref.shape[1], width).astype(bf16)
    picked = jnp.dot(lines, pick, preferred_element_type=f32)
    rows = lines_ref.shape[1]
    for m in range(chunks_ref.shape[0]):
        q, i = divmod(m, templ_here)
        chunks_ref[m] = picked[q * rows : (q + 1) * rows, i * LANES : (i + 1) * LANES]

    row = lax.broadcasted_iota(jnp.int32, (step, LANES), 0)
    inside = lax.broadcasted_iota(jnp.int32, (step, LANES), 1) % step <= row

    for c in range(channels_here):
        before = jnp.zeros((step, LANES), f32)
        for m in range(chunks):
            if m * step < length:
                line = jnp.broadcast_to(chunks_ref[m, c : c + 1, :], (step, LANES))
                here = pltpu.roll(line, LANES - step + 1, 1, stride=1, stride_axis=0)
                following = pltpu.roll(line, 1, 1, stride=1, stride_axis=0)
            else:
                here = following = jnp.zeros((step, LANES), f32)
            weights_ref[c, m * step : (m + 1) * step, :] = jnp.where(inside, here, before).astype(bf16)
            before = following
    for copy in small:
        copy.wait()
    coded_ref[...] = 2 * off_ref[...] + avail_ref[...]


def stack_kernel(
    coded_ref, inv_ref, records_ref, weights_ref, out_ref,
    picks_ref, pieces_ref, tails_ref, totals_ref, heads_ref, sem, *slots,
    length,
):
    templ_here, channels_here = coded_ref.shape
    step = LANES // templ_here
    blocks = tails_ref.shape[1]
    framed = slots[: len(slots) // 2]
    moved = slots[len(slots) // 2 :]
    pitch = records_ref.shape[0] // blocks
    lag_blocks = out_ref.shape[0] // templ_here
    taps = weights_ref.shape[1] // LANES
    bf16, f32 = jnp.bfloat16, jnp.float32
    picks = pltpu.make_async_copy(coded_ref, picks_ref, sem)
    picks.start()
    row = lax.broadcasted_iota(jnp.int32, (LANES, LANES), 0)
    col = lax.broadcasted_iota(jnp.int32, (LANES, LANES), 1)
    turn = LANES - length % LANES
    kinds = (row >= col, row >= 0, row < (col - turn) % LANES)
    adder = jnp.concatenate([kind.astype(f32) for kind in kinds], axis=1).astype(bf16)
    adder = jnp.concatenate([adder, adder], axis=0)

    picks.wait()

    def block_sums():
        for c in range(channels_here):
            x = records_ref[pl.ds(c, blocks, stride=pitch), :]
            for k, v in enumerate((x, x * x)):
                rows = pl.ds((2 * c + k) * blocks, blocks)
                high = v.astype(bf16)
                pieces_ref[rows, 0:LANES] = high
                pieces_ref[rows, LANES : 2 * LANES] = (v - high.astype(f32)).astype(bf16)
        sums = jnp.dot(pieces_ref[...], adder, preferred_element_type=f32)
        count = 2 * channels_here
        for k, ref in enumerate((tails_ref, totals_ref, heads_ref)):
            ref[:, :blocks, :] = sums[:, k * LANES : (k + 1) * LANES].reshape(count, blocks, LANES)
            if ref.shape[1] > blocks:
                ref[:, blocks:, :] = jnp.zeros((count, SUBLANES, LANES), f32)

    stacks = [jnp.zeros((lag_blocks, LANES), f32) for _ in range(templ_here)]
    for ref in framed:
        ref[blocks:, :] = jnp.zeros((SUBLANES, LANES), f32)

    whole = length // LANES
    lane = lax.broadcasted_iota(jnp.int32, (blocks, LANES), 1)
    lag_lane = lax.broadcasted_iota(jnp.int32, (lag_blocks, LANES), 1)

    def window_sum(index):
        def at(ref, i):
            return ref[index, i : i + blocks, :]

        total = at(tails_ref, 0)
        for i in range(1, whole):
            total = total + at(totals_ref, i)
        ends = jnp.where(lane < turn, at(heads_ref, whole), at(totals_ref, whole) + at(heads_ref, whole + 1))
        return total + ends

    def diagonals(arrays):
        count = len(arrays)
        moved_on = [arrays[0]] + [pltpu.roll(arrays[r], r * step, 1) for r in range(1, count)]
        block = lane // step
        out = []
        for t in range(count):
            line = moved_on[0]
            for r in range(1, count):
                line = jnp.where(block == (t + r) % count, moved_on[r], line)
            out.append(line)
        return out

    def regrouped(c):
        slot = c * templ_here
        here = records_ref[pl.ds(c, blocks, stride=pitch), :]
        framed[slot][:blocks, :] = here
        for r in range(1, templ_here):
            ref = framed[slot + r]
            turned = pltpu.roll(here, LANES - r * step, 1)
            ref[:blocks, :] = turned
            ref[:blocks, :] = jnp.where(lane < LANES - r * step, turned, ref[1 : blocks + 1, :])
        frames = jnp.concatenate(
            [
                jnp.concatenate([framed[slot + r][q : q + blocks, :].astype(bf16) for q in range(taps)], axis=1)
                for r in range(templ_here)
            ],
            axis=0,
        )
        product = jnp.dot(frames, weights_ref[c], preferred_element_type=f32) * inv_ref[c : c + 1, :]
        return diagonals([product[r * blocks : (r + 1) * blocks, :] for r in range(templ_here)])

    def picked(c, correlated, stacks):
        slot = c * templ_here
        first = window_sum(2 * c)
        second = window_sum(2 * c + 1)
        scale = lax.rsqrt(second - first * first / length + 1e-05)
        for t in range(templ_here):
            pick = picks_ref[t, c]
            down = pick >> LANE_BITS + 1
            over = (pick >> 1) & (LANES - 1)
            ref = moved[slot + t]
            turned = pltpu.roll(scale, t * step, 1) if t else scale
            ref[:blocks, :] = pltpu.roll(correlated[t] * turned, (2 * LANES - t * step - over) & (LANES - 1), 1)
            near = ref[pl.ds(down, lag_blocks), :]
            far = ref[pl.ds(down + 1, lag_blocks), :]
            lags = jnp.where(lag_lane < LANES - over, near, far)
            stacks[t] = stacks[t] + lags * (pick & 1).astype(f32)

    block_sums()
    ahead = regrouped(0)
    for c in range(channels_here):
        ready, ahead = ahead, regrouped(c + 1) if c + 1 < channels_here else None
        picked(c, ready, stacks)

    for t in range(templ_here):
        out_ref[t * lag_blocks : (t + 1) * lag_blocks, :] = stacks[t]


def finish_kernel(place_ref, *refs):
    *parts, out_ref, stack_ref = refs
    templ_here, share = out_ref.shape
    lag_blocks = stack_ref.shape[0] // templ_here
    own = share // LANES
    for t in range(templ_here):
        rows = pl.ds(t * lag_blocks, lag_blocks)
        stack = parts[0][rows, :].astype(jnp.float32)
        for part in parts[1:]:
            stack = stack + part[rows, :].astype(jnp.float32)
        stack_ref[rows, :] = stack
        power = jnp.sum(jnp.sum(stack * stack, axis=0, keepdims=True), axis=1, keepdims=True)
        unit = 1.0 / jnp.sqrt(power / (lag_blocks * LANES) + 1e-05)
        for i in range(own):
            line = stack_ref[pl.ds(t * lag_blocks + place_ref[0] * own + i, 1), :]
            out_ref[t : t + 1, i * LANES : (i + 1) * LANES] = line * unit


def spread_kernel(records_ref, out_ref):
    channels_here = records_ref.shape[0]
    block = records_ref[...]
    for i in range(out_ref.shape[0] // channels_here):
        out_ref[i * channels_here : (i + 1) * channels_here, :] = block


def spread_records(records, count):
    channels_here, block_len = records.shape
    copies = pl.pallas_call(
        spread_kernel,
        out_shape=jax.ShapeDtypeStruct((count * channels_here, block_len), records.dtype),
        in_specs=[VMEM],
        out_specs=VMEM,
        compiler_params=limit(2),
        name="spread_records",
    )(records)
    return copies.reshape(count, channels_here, 1, block_len)


def prepared_weights(templates, offsets, available):
    templ_here, channels_here, length = templates.shape
    step = LANES // templ_here
    groups = -(-length // LANES)
    rows = padded_rows(channels_here)
    lines = pltpu.VMEM((groups, rows, templ_here * LANES), jnp.float32)
    chunks = pltpu.VMEM((groups * templ_here, rows, LANES), jnp.float32)
    return pl.pallas_call(
        weights_kernel,
        out_shape=(
            jax.ShapeDtypeStruct((channels_here, chunks_of(length, step) * step, LANES), jnp.bfloat16),
            jax.ShapeDtypeStruct((channels_here, LANES), jnp.float32),
            jax.ShapeDtypeStruct(offsets.shape, jnp.int32),
        ),
        in_specs=[HBM, HBM, VMEM],
        out_specs=(VMEM, VMEM, VMEM),
        scratch_shapes=[
            pltpu.VMEM(offsets.shape, jnp.int32),
            pltpu.VMEM(offsets.shape, jnp.int32),
            lines,
            chunks,
            pltpu.SemaphoreType.DMA((2,)),
        ],
        compiler_params=limit(16),
        name="prepare_weights",
    )(*(pltpu.with_memory_space_constraint(a, pltpu.HBM) for a in (offsets, available)), templates)


def partial_stacks(blocks, count, weights, inv, coded, lag_count, length):
    templ_here, channels_here = coded.shape
    lag_blocks = lag_count // LANES
    total_rows = 2 * channels_here * count
    f32 = jnp.float32
    return pl.pallas_call(
        lambda *refs: stack_kernel(*refs, length=length),
        out_shape=jax.ShapeDtypeStruct((templ_here * lag_blocks, LANES), f32),
        in_specs=[VMEM, VMEM, VMEM, VMEM],
        out_specs=VMEM,
        scratch_shapes=[
            pltpu.SMEM(coded.shape, coded.dtype),
            pltpu.VMEM((total_rows, 2 * LANES), jnp.bfloat16),
            pltpu.VMEM((2 * channels_here, count, LANES), f32),
            pltpu.VMEM((2 * channels_here, count + SUBLANES, LANES), f32),
            pltpu.VMEM((2 * channels_here, count + SUBLANES, LANES), f32),
            pltpu.SemaphoreType.DMA(()),
        ]
        + [pltpu.VMEM((count + SUBLANES, LANES), f32)] * (2 * channels_here * templ_here),
        compiler_params=limit(24),
        name="stack_channels",
    )(coded, inv, blocks, weights)


def finished(place, parts, templ_here, share):
    return pl.pallas_call(
        finish_kernel,
        out_shape=jax.ShapeDtypeStruct((templ_here, share), jnp.float32),
        in_specs=[SMEM] + [VMEM] * len(parts),
        out_specs=VMEM,
        scratch_shapes=[pltpu.VMEM(parts[0].shape, jnp.float32)],
        compiler_params=limit(4),
        name="finish",
    )(place, *parts)


ORDER = (1, 2, 6)


def swapped(array, distance):
    return lax.ppermute(array, "sta", [(i, i ^ distance) for i in range(lax.axis_size("sta"))])


def shards(records, templates, offsets, available):
    block_len = records.shape[1]
    templ_here, _, length = templates.shape
    count = lax.axis_size("tmpl")
    shares = lax.axis_size("sta")
    lag_count = block_len * count - OFFMAX - length + 1
    blocks = lax.all_to_all(spread_records(records, count), "tmpl", 0, 0, tiled=True)
    weights, inv, coded = prepared_weights(templates, offsets, available)
    mine = partial_stacks(blocks.reshape(-1, block_len), count, weights, inv, coded, lag_count, length)
    place = lax.axis_index("sta").reshape(1).astype(jnp.int32)
    bf16, f32 = jnp.bfloat16, jnp.float32
    parts = [mine]
    for distance in ORDER:
        mine = parts[0] if len(parts) == 1 else parts[0] + parts[1].astype(f32)
        parts = [mine, swapped(mine if distance == 1 else mine.astype(bf16), distance)]
    return finished(place, parts, templ_here, lag_count // shares)


def solution(mesh):
    in_specs = (P("sta", "tmpl"), P("tmpl", "sta", None), P("tmpl", "sta"), P("tmpl", "sta"))
    out_specs = P("tmpl", "sta")
    return jax.shard_map(shards, mesh=mesh, in_specs=in_specs, out_specs=out_specs, check_vma=False)
```
